256 devices in a mesh: row: 128 (over z, y_lo, x, core), ch: 2 (over y_hi).
Axes of the slice: x: 4, y: 4 (y_hi: 2, y_lo: 2; y = y_hi * 2 + y_lo), z: 8, core: 2. Of those that a mesh axis runs over, the one named last changes fastest.
Arguments:
- pair_rep: bfloat16 [384, 384, 128], P('row'), may hold values from -6 to 6
- res_mask: int32 [384], replicated, may hold values 0 or 1
- in_gain: float32 [128], replicated, may hold values from 0.5 to 1.5
- w_left: bfloat16 [128, 128], P(None, 'ch'), may hold values from -0.5 to 0.5
- w_left_gate: bfloat16 [128, 128], P(None, 'ch'), may hold values from -0.5 to 0.5
- w_right: bfloat16 [128, 128], P(None, 'ch'), may hold values from -0.5 to 0.5
- w_right_gate: bfloat16 [128, 128], P(None, 'ch'), may hold values from -0.5 to 0.5
- w_gate: bfloat16 [128, 128], replicated, may hold values from -0.5 to 0.5
- mid_gain: float32 [128], replicated, may hold values from 0.5 to 1.5
- w_out: bfloat16 [128, 128], replicated, may hold values from -0.5 to 0.5
- next_gain: float32 [128], replicated, may hold values from 0.5 to 1.5
Outputs:
- new_pair: bfloat16 [384, 384, 128], P(None, 'row', 'ch')
- new_norm: bfloat16 [384, 384, 128], P(None, 'row', 'ch')
The draws below stay inside these ranges and needn't reach their ends.
All inputs are finite; a program needn't handle non-finite values.
Results may differ from the reference program's by a relative error of at most 0.0065.
Values may be sent and summed in bfloat16 or wider, within the bound.
A program may use at most 64 MiB of HBM per device.

```python
import jax
import jax.numpy as jnp
from jax import lax

C = 128
H = 128
N = 384


def set_ends(drawn, own_key, low, top_value):
    index_at = [jax.random.randint(jax.random.fold_in(own_key, axis), (), 0, length) for axis, length in enumerate(drawn.shape)]
    longest = drawn.shape.index(max(drawn.shape))
    next_to = index_at[:longest] + [(index_at[longest] + 1) % drawn.shape[longest]] + index_at[longest + 1:]
    return drawn.at[tuple(index_at)].set(low).at[tuple(next_to)].set(top_value)


def shard_levels(stream_key, extent, pieces, low, high):
    loudness, own = 1.0, jax.random.fold_in(stream_key, 6)
    for position, blocks in pieces:
        draws = jnp.exp(jax.random.uniform(jax.random.fold_in(own, position), (blocks,), jnp.float32, low / len(pieces), high / len(pieces)))
        loudness = loudness * jnp.repeat(draws, extent[position] // blocks).reshape([-1 if axis == position else 1 for axis in range(len(extent))])
    return loudness


def bell_draw(own_key, extent, scale, limit, shards=(), held_as=jnp.bfloat16):
    factor_of = shard_levels(own_key, extent, shards, -0.22, 0.18) if shards else 1.0
    result = jax.random.normal(own_key, extent, jnp.float32) * scale * factor_of
    return jnp.minimum(jnp.maximum(result, -limit), limit).astype(held_as)


def setup_inputs(seed: int = 0) -> dict:
    arg_keys = jax.random.split(jax.random.key(seed), 12)
    pair_rep = bell_draw(arg_keys[0], (N, N, C), 1.0, 6.0, ((0, 128),))
    res_mask = set_ends((jax.random.randint(arg_keys[1], (N,), 0, 8) < 7).astype(jnp.int32), jax.random.fold_in(arg_keys[1], 1), 0, 1)
    in_gain = jnp.clip(1.0 + 0.1 * jax.random.normal(arg_keys[2], (C,), jnp.float32), 0.5, 1.5)
    w_left = bell_draw(arg_keys[3], (C, H), C ** -0.5, 0.5, ((1, 2),))
    w_left_gate = bell_draw(arg_keys[4], (C, H), C ** -0.5, 0.5, ((1, 2),))
    w_right = bell_draw(arg_keys[5], (C, H), C ** -0.5, 0.5, ((1, 2),))
    w_right_gate = bell_draw(arg_keys[6], (C, H), C ** -0.5, 0.5, ((1, 2),))
    w_gate = bell_draw(arg_keys[7], (C, C), C ** -0.5, 0.5)
    mid_gain = jnp.clip(1.0 + 0.1 * jax.random.normal(arg_keys[8], (H,), jnp.float32), 0.5, 1.5)
    w_out = bell_draw(arg_keys[9], (H, C), H ** -0.5, 0.5)
    next_gain = jnp.clip(1.0 + 0.1 * jax.random.normal(arg_keys[10], (C,), jnp.float32), 0.5, 1.5)
    return dict(pair_rep=pair_rep, res_mask=res_mask, in_gain=in_gain, w_left=w_left, w_left_gate=w_left_gate, w_right=w_right, w_right_gate=w_right_gate, w_gate=w_gate, mid_gain=mid_gain, w_out=w_out, next_gain=next_gain)


def normalize(values, scale_gain, along):
    values = values.astype(jnp.float32)
    average = lax.optimization_barrier(jnp.mean(values, along, keepdims=True))
    centred = values - average
    spread = lax.optimization_barrier(jnp.mean(centred * centred, along, keepdims=True))
    return centred * lax.rsqrt(spread + 1e-05) * scale_gain

def reference(pair_rep, res_mask, in_gain, w_left, w_left_gate, w_right, w_right_gate, w_gate, mid_gain, w_out, next_gain):
    res_float = res_mask.astype(jnp.float32)
    pair_mask = res_float[:, None] * res_float[None, :]
    normed = normalize(pair_rep, in_gain, 2).astype(jnp.bfloat16)
    normed_wide = normed.astype(jnp.float32)

    def project(weight, weight_gate):
        values_lin = jnp.einsum('ilc,ch->hil', normed_wide, weight.astype(jnp.float32))
        switch = jnp.einsum('ilc,ch->hil', normed_wide, weight_gate.astype(jnp.float32))
        return (jax.nn.sigmoid(switch) * values_lin * pair_mask[None]).astype(jnp.bfloat16)
    left_side = project(w_left, w_left_gate)
    right_side = project(w_right, w_right_gate)
    triangle = jnp.einsum('kil,kjl->kij', left_side.astype(jnp.float32), right_side.astype(jnp.float32))
    tri_normed = normalize(triangle, mid_gain[:, None, None], 0).astype(jnp.bfloat16)
    update = jnp.einsum('kij,kc->ijc', tri_normed.astype(jnp.float32), w_out.astype(jnp.float32))
    gate_vals = jax.nn.sigmoid(jnp.einsum('ijc,cd->ijd', normed_wide, w_gate.astype(jnp.float32)))
    new_pair = (pair_rep.astype(jnp.float32) + gate_vals * update).astype(jnp.bfloat16)
    new_norm = normalize(new_pair, next_gain, 2).astype(jnp.bfloat16)
    return (new_pair, new_norm)
```

```python
import functools

import jax
import jax.numpy as jnp
from jax import lax
from jax.experimental import pallas as pl
from jax.experimental.pallas import tpu as pltpu
from jax.sharding import PartitionSpec as P

EPS = 1e-05
F32 = jnp.float32
BF16 = jnp.bfloat16
GROUPS = 4


def dot(a, b, ca, cb):
    return lax.dot_general(a, b, (((ca,), (cb,)), ((), ())), preferred_element_type=F32)


def iota(shape, dim):
    return lax.broadcasted_iota(jnp.int32, shape, dim)


def one_hot(cond):
    return jnp.where(cond, 1.0, 0.0).astype(BF16)


def normalize(v, gain):
    scale = 1.0 / v.shape[1]
    centred = v - jnp.sum(v, 1, keepdims=True) * scale
    var = jnp.sum(centred * centred, 1, keepdims=True) * scale
    return centred * lax.rsqrt(var + EPS) * gain


def kernel(
    rows_n,
    x_ref,
    mask_smem,
    mask_row,
    in_gain,
    wl,
    wlg,
    wr,
    wrg,
    wg,
    mid_gain,
    wo,
    next_gain,
    out_pair,
    out_norm,
    sa,
    d,
    ps,
    pb,
    sc,
    q,
    gate_buf,
    pair_buf,
    sem_a_send,
    sem_a_recv,
    sem_f_send,
    sem_f_recv,
    sem_p_send,
    sem_p_recv,
    sem_c_send,
    sem_c_recv,
):
    r_n = rows_n
    k_n = r_n // 2
    n = 3 * r_n
    b = r_n
    chans = x_ref.shape[1]
    half = chans // 2
    me = lax.axis_index("row")
    c = lax.axis_index("ch")
    core = lax.rem(me, 2)
    slot = me // 2
    per = k_n // GROUPS

    barrier = pltpu.get_barrier_semaphore()

    def greet_own(t, carry):
        pl.semaphore_signal(barrier, inc=1, device_id={"row": lax.rem(me + t, r_n), "ch": c})
        return carry

    def greet_other(t, carry):
        s = lax.rem(slot + t, k_n)
        pl.semaphore_signal(barrier, inc=1, device_id={"row": 2 * s + core, "ch": 1 - c})
        return carry

    lax.fori_loop(1, r_n, greet_own, 0)
    lax.fori_loop(0, k_n, greet_other, 0)

    hl = wl.shape[1]
    p_row, p_col = iota((2 * hl, hl), 0), iota((2 * hl, hl), 1)
    to_left, to_right = one_hot(p_row == 2 * p_col), one_hot(p_row == 2 * p_col + 1)
    w_lin = (dot(to_left, wl[...], 1, 1) + dot(to_right, wr[...], 1, 1)).astype(BF16)
    w_switch = (dot(to_left, wlg[...], 1, 1) + dot(to_right, wrg[...], 1, 1)).astype(BF16)
    for i in range(3):
        normed = normalize(x_ref[i * n : (i + 1) * n].astype(F32), in_gain[...]).astype(BF16)
        lin = dot(w_lin, normed, 1, 1)
        switch = dot(w_switch, normed, 1, 1)
        mask = mask_row[...].astype(F32) * mask_smem[3 * me + i].astype(F32)
        sides = (jax.nn.sigmoid(switch) * lin * mask).astype(BF16)
        for lb in range(3):
            sa[:, lb, i] = sides[:, lb * b : (lb + 1) * b].reshape(hl, 2, b)

    pl.semaphore_wait(barrier, r_n - 1 + k_n)

    group = slot // per

    def send_a(t, carry):
        s = lax.rem(slot + t, k_n)
        pltpu.make_async_remote_copy(
            src_ref=sa.at[s],
            dst_ref=d.at[core, :, slot],
            send_sem=sem_a_send,
            recv_sem=sem_a_recv.at[group],
            device_id={"row": 2 * s + core, "ch": c},
        ).start()
        return carry

    lax.fori_loop(1, k_n, send_a, 0)
    pltpu.make_async_copy(sa.at[slot], d.at[core, :, slot], sem_a_recv.at[group]).start()

    p_row, p_col = iota((2 * r_n, 2 * n), 0), iota((2 * r_n, 2 * n), 1)
    first = (p_row & 1) * n + 3 * (p_row >> 1)
    for j in range(3):
        rows = dot(one_hot(p_col == first + j), x_ref[0 : 2 * n], 1, 0)
        ps[j] = rows.astype(BF16).reshape(r_n, 2, chans)
    p_row, p_col = iota((2 * r_n, n), 0), iota((2 * r_n, n), 1)
    last = x_ref[2 * n : 3 * n]
    rows = dot(one_hot(p_col == 3 * (p_row >> 1) + (p_row & 1)), last, 1, 0)
    ps[3] = rows.astype(BF16).reshape(r_n, 2, chans)
    rows = dot(one_hot(p_col == 3 * (p_row >> 1) + 2), last, 1, 0)
    ps[4] = rows.astype(BF16).reshape(r_n, 2, chans)

    def send_p(t, carry):
        r = lax.rem(me + t, r_n)
        pltpu.make_async_remote_copy(
            src_ref=ps.at[:, r],
            dst_ref=pb.at[:, me],
            send_sem=sem_p_send,
            recv_sem=sem_p_recv,
            device_id={"row": r, "ch": c},
        ).start()
        return carry

    lax.fori_loop(1, r_n, send_p, 0)
    pltpu.make_async_copy(ps.at[:, me], pb.at[:, me], sem_p_recv).start()

    s_row, s_col = iota((n, n), 0), iota((n, n), 1)
    sixth = (s_col * 10923) >> 16
    left_at = 6 * sixth + ((s_col - 6 * sixth) >> 1)
    is_left = (s_col & 1) == 0
    sel_left = [one_hot((s_row == left_at + 3 * h) & is_left) for h in range(2)]
    s_row, s_col = iota((2 * r_n, n), 0), iota((2 * r_n, n), 1)
    in_two = s_row < r_n
    s_two = jnp.where(in_two, s_row, s_row - r_n)
    sel_right = one_hot(
        s_col == 6 * (s_two >> 1) + jnp.where(in_two, 2 * (s_two & 1) + 1, 5)
    )

    other = {"row": 2 * slot + 1 - core, "ch": c}
    for g in range(GROUPS):
        part = d.at[core, :, g * per : (g + 1) * per]
        pltpu.make_async_copy(part, part, sem_a_recv.at[g]).wait()
        pltpu.make_async_remote_copy(
            src_ref=part,
            dst_ref=part,
            send_sem=sem_f_send,
            recv_sem=sem_f_recv.at[g],
            device_id=other,
        ).start()
    for g in range(GROUPS):
        part = d.at[1 - core, :, g * per : (g + 1) * per]
        pltpu.make_async_copy(part, part, sem_f_recv.at[g]).wait()

    lefts, rights = [], []
    for lb in range(3):
        acc = dot(sel_left[0], d[0, lb].reshape(2 * n // 2, b), 1, 0)
        acc = acc + dot(sel_left[1], d[1, lb].reshape(2 * n // 2, b), 1, 0)
        lefts.append(acc.astype(BF16))
        rights.append(dot(sel_right, d[core, lb].reshape(n, b), 1, 0).astype(BF16))
    triangle = dot(jnp.concatenate(rights, 1), jnp.concatenate(lefts, 1), 1, 1)
    upper, lower = triangle[:r_n], triangle[r_n:]
    for ib in range(3):
        sc[ib] = upper[:, ib * b : (ib + 1) * b].astype(BF16).reshape(k_n, 2, b)
    odd = (iota((r_n, b), 0) & 1) == 1
    sc[3] = jnp.where(odd, lower[:, b : 2 * b], lower[:, :b]).astype(BF16).reshape(k_n, 2, b)
    sc[4] = lower[:, 2 * b :].astype(BF16).reshape(k_n, 2, b)

    k_me = c * k_n + slot

    def send_c(t, carry):
        s = lax.rem(slot + t, k_n)
        pltpu.make_async_remote_copy(
            src_ref=sc.at[:, s],
            dst_ref=q.at[:, k_me],
            send_sem=sem_c_send.at[0],
            recv_sem=sem_c_recv,
            device_id={"row": 2 * s + core, "ch": c},
        ).start()
        return carry

    def send_c_other(t, carry):
        s = lax.rem(slot + t, k_n)
        pltpu.make_async_remote_copy(
            src_ref=sc.at[:, s],
            dst_ref=q.at[:, k_me],
            send_sem=sem_c_send.at[1],
            recv_sem=sem_c_recv,
            device_id={"row": 2 * s + core, "ch": 1 - c},
        ).start()
        return carry

    lax.fori_loop(0, k_n, send_c_other, 0)
    lax.fori_loop(1, k_n, send_c, 0)
    pltpu.make_async_copy(sc.at[:, slot], q.at[:, k_me], sem_c_recv).start()

    pltpu.make_async_copy(pb, pb, sem_p_recv).wait()
    s_row, s_col = iota((n, 2 * r_n), 0), iota((n, 2 * r_n), 1)
    sel_two = one_hot(s_row == 3 * (s_col >> 1) + (s_col & 1))
    third = s_row == 3 * (s_col >> 1) + 2
    sel_last = [one_hot(third & ((s_col & 1) == s)) for s in range(2)]
    for j in range(3):
        rest = pb[3 + j // 2].reshape(2 * r_n, chans)
        cells = dot(sel_two, pb[j].reshape(2 * r_n, chans), 1, 0) + dot(sel_last[j % 2], rest, 1, 0)
        pair_buf[j] = cells
        normed = normalize(cells, in_gain[...]).astype(BF16)
        gate_buf[j] = jax.nn.sigmoid(dot(normed, wg[...], 1, 0))

    hidden = wo.shape[0]
    p_row, p_col = iota((2 * hidden, hidden), 0), iota((2 * hidden, hidden), 1)
    twice = (p_row >> 1) == p_col
    gain_col = jnp.sum(jnp.where(twice, mid_gain[...], 0.0), 1, keepdims=True)
    w_twice = dot(one_hot(twice), wo[...], 1, 0)
    even = (iota((2 * hidden, chans), 0) & 1) == 0
    w_out = jnp.concatenate(
        [jnp.where(even, w_twice, 0.0), jnp.where(even, 0.0, w_twice)], 1
    ).astype(BF16)
    gain_all = jnp.broadcast_to(gain_col, (2 * hidden, b))

    pltpu.make_async_copy(q, q, sem_c_recv).wait()

    def total(v):
        t = jnp.sum(v.reshape(2 * hidden // 8, 8, b), 0)
        t = t + pltpu.roll(t, 4, 0)
        t = t + pltpu.roll(t, 2, 0)
        return jnp.broadcast_to(t[None], (2 * hidden // 8, 8, b)).reshape(2 * hidden, b)

    def finish(j, ib, update):
        span = slice(ib * b, (ib + 1) * b)
        new = (pair_buf[j, span] + gate_buf[j, span] * update).astype(BF16)
        values = new.astype(F32)
        normed = normalize(values, next_gain[...])
        second = c == 1
        out_pair[j, span] = jnp.where(second, values[:, half:], values[:, :half]).astype(BF16)
        out_norm[j, span] = jnp.where(second, normed[:, half:], normed[:, :half]).astype(BF16)

    for w in range(5):
        t = q[w].reshape(2 * hidden, b).astype(F32)
        centred = t - total(t) * (1.0 / hidden)
        var = total(centred * centred) * (1.0 / hidden)
        tri = (centred * lax.rsqrt(var + EPS) * gain_all).astype(BF16)
        update = dot(tri, w_out, 0, 0)
        if w < 3:
            finish(0, w, update[:, :chans])
            finish(1, w, update[:, chans:])
        elif w == 3:
            finish(2, 0, update[:, :chans])
            finish(2, 1, update[:, chans:])
        else:
            finish(2, 2, update[:, :chans])

    part = sa.at[0 : k_n - 1]
    pltpu.make_async_copy(part, part, sem_a_send).wait()
    part = d.at[core]
    pltpu.make_async_copy(part, part, sem_f_send).wait()
    part = ps.at[:, 0 : r_n - 1]
    pltpu.make_async_copy(part, part, sem_p_send).wait()
    part = sc.at[:, 0 : k_n - 1]
    pltpu.make_async_copy(part, part, sem_c_send.at[0]).wait()
    pltpu.make_async_copy(sc, sc, sem_c_send.at[1]).wait()


def local(
    r_n,
    pair_rep,
    res_mask,
    in_gain,
    w_left,
    w_left_gate,
    w_right,
    w_right_gate,
    w_gate,
    mid_gain,
    w_out,
    next_gain,
):
    rows, n, chans = pair_rep.shape
    k_n = r_n // 2
    half = chans // 2
    vmem = pl.BlockSpec(memory_space=pltpu.VMEM)
    smem = pl.BlockSpec(memory_space=pltpu.SMEM)
    dma = pltpu.SemaphoreType.DMA
    out = jax.ShapeDtypeStruct((3, n, half), BF16)
    new_pair, new_norm = pl.pallas_call(
        functools.partial(kernel, r_n),
        out_shape=(out, out),
        in_specs=[vmem, smem] + [vmem] * 10,
        out_specs=(vmem, vmem),
        scratch_shapes=[
            pltpu.VMEM((k_n, 3, 3, 2, r_n), BF16),
            pltpu.VMEM((2, 3, k_n, 3, 2, r_n), BF16),
            pltpu.VMEM((5, r_n, 2, chans), BF16),
            pltpu.VMEM((5, r_n, 2, chans), BF16),
            pltpu.VMEM((5, k_n, 2, r_n), BF16),
            pltpu.VMEM((5, r_n, 2, r_n), BF16),
            pltpu.VMEM((3, n, chans), F32),
            pltpu.VMEM((3, n, chans), F32),
            dma,
            dma((GROUPS,)),
            dma,
            dma((GROUPS,)),
            dma,
            dma,
            dma((2,)),
            dma,
        ],
        compiler_params=pltpu.CompilerParams(collective_id=0, has_side_effects=True),
    )(
        pair_rep.reshape(rows * n, chans),
        res_mask,
        res_mask.reshape(1, n),
        in_gain.reshape(1, chans),
        w_left,
        w_left_gate,
        w_right,
        w_right_gate,
        w_gate,
        mid_gain.reshape(1, -1),
        w_out,
        next_gain.reshape(1, chans),
    )
    return jnp.transpose(new_pair, (1, 0, 2)), jnp.transpose(new_norm, (1, 0, 2))


def solution(mesh):
    return jax.shard_map(
        functools.partial(local, mesh.shape["row"]),
        mesh=mesh,
        in_specs=(
            P("row", None, None),
            P(),
            P(),
            P(None, "ch"),
            P(None, "ch"),
            P(None, "ch"),
            P(None, "ch"),
            P(),
            P(),
            P(),
            P(),
        ),
        out_specs=(P(None, "row", "ch"), P(None, "row", "ch")),
        check_vma=False,
    )
```

```python
import functools

import jax
import jax.numpy as jnp
from jax import lax
from jax.experimental import pallas as pl
from jax.experimental.pallas import tpu as pltpu
from jax.sharding import PartitionSpec as P

EPS = 1e-05
F32 = jnp.float32
BF16 = jnp.bfloat16
GROUPS = 4


def dot(a, b, ca, cb):
    return lax.dot_general(a, b, (((ca,), (cb,)), ((), ())), preferred_element_type=F32)


def iota(shape, dim):
    return lax.broadcasted_iota(jnp.int32, shape, dim)


def one_hot(cond):
    return jnp.where(cond, 1.0, 0.0).astype(BF16)


def to_column(row):
    size = row.shape[1]
    diagonal = iota((size, size), 0) == iota((size, size), 1)
    return jnp.sum(jnp.where(diagonal, row, 0.0), 1, keepdims=True)


def normalize(v, gain, along):
    scale = 1.0 / v.shape[along]
    centred = v - jnp.sum(v, along, keepdims=True) * scale
    var = jnp.sum(centred * centred, along, keepdims=True) * scale
    return centred * lax.rsqrt(var + EPS) * gain


def kernel(
    rows_n,
    x_ref,
    mask_smem,
    mask_row,
    in_gain,
    wl,
    wlg,
    wr,
    wrg,
    wg,
    mid_gain,
    wo,
    next_gain,
    out_pair,
    out_norm,
    sa,
    d,
    ps,
    pb,
    sc,
    q,
    gate_buf,
    pair_buf,
    sem_a_send,
    sem_a_recv,
    sem_f_send,
    sem_f_recv,
    sem_p_send,
    sem_p_recv,
    sem_c_send,
    sem_c_recv,
):
    r_n = rows_n
    k_n = r_n // 2
    n = 3 * r_n
    b = r_n
    chans = x_ref.shape[1]
    half = chans // 2
    me = lax.axis_index("row")
    c = lax.axis_index("ch")
    core = lax.rem(me, 2)
    slot = me // 2
    per = k_n // GROUPS

    barrier = pltpu.get_barrier_semaphore()

    def greet_own(t, carry):
        pl.semaphore_signal(barrier, inc=1, device_id={"row": lax.rem(me + t, r_n), "ch": c})
        return carry

    def greet_other(t, carry):
        s = lax.rem(slot + t, k_n)
        pl.semaphore_signal(barrier, inc=1, device_id={"row": 2 * s + core, "ch": 1 - c})
        return carry

    lax.fori_loop(1, r_n, greet_own, 0)
    lax.fori_loop(0, k_n, greet_other, 0)

    hl = wl.shape[0]
    p_row, p_col = iota((2 * hl, hl), 0), iota((2 * hl, hl), 1)
    to_left, to_right = one_hot(p_row == 2 * p_col), one_hot(p_row == 2 * p_col + 1)
    w_lin = (dot(to_left, wl[...], 1, 0) + dot(to_right, wr[...], 1, 0)).astype(BF16)
    w_switch = (dot(to_left, wlg[...], 1, 0) + dot(to_right, wrg[...], 1, 0)).astype(BF16)
    for i in range(3):
        normed = normalize(x_ref[i * n : (i + 1) * n].astype(F32), in_gain[...], 1).astype(BF16)
        lin = dot(w_lin, normed, 1, 1)
        switch = dot(w_switch, normed, 1, 1)
        mask = mask_row[...].reshape(1, n).astype(F32) * mask_smem[3 * me + i].astype(F32)
        sides = (jax.nn.sigmoid(switch) * lin * mask).astype(BF16)
        for lb in range(3):
            sa[:, lb, i] = sides[:, lb * b : (lb + 1) * b].reshape(hl, 2, b)

    pl.semaphore_wait(barrier, r_n - 1 + k_n)

    group = slot // per

    def send_a(t, carry):
        s = lax.rem(slot + t, k_n)
        pltpu.make_async_remote_copy(
            src_ref=sa.at[s],
            dst_ref=d.at[core, :, slot],
            send_sem=sem_a_send,
            recv_sem=sem_a_recv.at[group],
            device_id={"row": 2 * s + core, "ch": c},
        ).start()
        return carry

    lax.fori_loop(1, k_n, send_a, 0)
    pltpu.make_async_copy(sa.at[slot], d.at[core, :, slot], sem_a_recv.at[group]).start()

    p_row, p_col = iota((2 * r_n, 2 * n), 0), iota((2 * r_n, 2 * n), 1)
    first = (p_row & 1) * n + 3 * (p_row >> 1)
    for j in range(3):
        rows = dot(one_hot(p_col == first + j), x_ref[0 : 2 * n], 1, 0)
        ps[j] = rows.astype(BF16).reshape(r_n, 2, chans)
    p_row, p_col = iota((2 * r_n, n), 0), iota((2 * r_n, n), 1)
    last = x_ref[2 * n : 3 * n]
    rows = dot(one_hot(p_col == 3 * (p_row >> 1) + (p_row & 1)), last, 1, 0)
    ps[3] = rows.astype(BF16).reshape(r_n, 2, chans)
    rows = dot(one_hot(p_col == 3 * (p_row >> 1) + 2), last, 1, 0)
    ps[4] = rows.astype(BF16).reshape(r_n, 2, chans)

    def send_p(t, carry):
        r = lax.rem(me + t, r_n)
        pltpu.make_async_remote_copy(
            src_ref=ps.at[:, r],
            dst_ref=pb.at[:, me],
            send_sem=sem_p_send,
            recv_sem=sem_p_recv,
            device_id={"row": r, "ch": c},
        ).start()
        return carry

    lax.fori_loop(1, r_n, send_p, 0)
    pltpu.make_async_copy(ps.at[:, me], pb.at[:, me], sem_p_recv).start()

    s_row, s_col = iota((n, n), 0), iota((n, n), 1)
    sixth = (s_col * 10923) >> 16
    left_at = 6 * sixth + ((s_col - 6 * sixth) >> 1)
    is_left = (s_col & 1) == 0
    sel_left = [one_hot((s_row == left_at + 3 * h) & is_left) for h in range(2)]
    s_row, s_col = iota((2 * r_n, n), 0), iota((2 * r_n, n), 1)
    in_two = s_row < r_n
    s_two = jnp.where(in_two, s_row, s_row - r_n)
    sel_right = one_hot(
        s_col == 6 * (s_two >> 1) + jnp.where(in_two, 2 * (s_two & 1) + 1, 5)
    )

    other = {"row": 2 * slot + 1 - core, "ch": c}
    for g in range(GROUPS):
        part = d.at[core, :, g * per : (g + 1) * per]
        pltpu.make_async_copy(part, part, sem_a_recv.at[g]).wait()
        pltpu.make_async_remote_copy(
            src_ref=part,
            dst_ref=part,
            send_sem=sem_f_send,
            recv_sem=sem_f_recv.at[g],
            device_id=other,
        ).start()
    for g in range(GROUPS):
        part = d.at[1 - core, :, g * per : (g + 1) * per]
        pltpu.make_async_copy(part, part, sem_f_recv.at[g]).wait()

    lefts, rights = [], []
    for lb in range(3):
        acc = dot(sel_left[0], d[0, lb].reshape(2 * n // 2, b), 1, 0)
        acc = acc + dot(sel_left[1], d[1, lb].reshape(2 * n // 2, b), 1, 0)
        lefts.append(acc.astype(BF16))
        rights.append(dot(sel_right, d[core, lb].reshape(n, b), 1, 0).astype(BF16))
    triangle = dot(jnp.concatenate(rights, 1), jnp.concatenate(lefts, 1), 1, 1)
    upper, lower = triangle[:r_n], triangle[r_n:]
    for ib in range(3):
        sc[ib] = upper[:, ib * b : (ib + 1) * b].astype(BF16).reshape(k_n, 2, b)
    odd = (iota((r_n, b), 0) & 1) == 1
    sc[3] = jnp.where(odd, lower[:, b : 2 * b], lower[:, :b]).astype(BF16).reshape(k_n, 2, b)
    sc[4] = lower[:, 2 * b :].astype(BF16).reshape(k_n, 2, b)

    k_me = c * k_n + slot

    def send_c(t, carry):
        s = lax.rem(slot + t, k_n)
        pltpu.make_async_remote_copy(
            src_ref=sc.at[:, s],
            dst_ref=q.at[:, k_me],
            send_sem=sem_c_send.at[0],
            recv_sem=sem_c_recv,
            device_id={"row": 2 * s + core, "ch": c},
        ).start()
        return carry

    def send_c_other(t, carry):
        s = lax.rem(slot + t, k_n)
        pltpu.make_async_remote_copy(
            src_ref=sc.at[:, s],
            dst_ref=q.at[:, k_me],
            send_sem=sem_c_send.at[1],
            recv_sem=sem_c_recv,
            device_id={"row": 2 * s + core, "ch": 1 - c},
        ).start()
        return carry

    lax.fori_loop(0, k_n, send_c_other, 0)
    lax.fori_loop(1, k_n, send_c, 0)
    pltpu.make_async_copy(sc.at[:, slot], q.at[:, k_me], sem_c_recv).start()

    pltpu.make_async_copy(pb, pb, sem_p_recv).wait()
    s_row, s_col = iota((2 * r_n, n), 0), iota((2 * r_n, n), 1)
    sel_two = one_hot(s_col == 3 * (s_row >> 1) + (s_row & 1))
    third = s_col == 3 * (s_row >> 1) + 2
    sel_last = [one_hot(third & ((s_row & 1) == s)) for s in range(2)]
    gain_c = to_column(in_gain[...])
    for j in range(3):
        rest = pb[3 + j // 2].reshape(2 * r_n, chans)
        cells = dot(pb[j].reshape(2 * r_n, chans), sel_two, 0, 0) + dot(rest, sel_last[j % 2], 0, 0)
        pair_buf[j] = cells
        normed = normalize(cells, gain_c, 0).astype(BF16)
        gate_buf[j] = jax.nn.sigmoid(dot(wg[...], normed, 0, 0))

    hidden = wo.shape[0]
    p_row, p_col = iota((2 * hidden, hidden), 0), iota((2 * hidden, hidden), 1)
    twice = (p_row >> 1) == p_col
    gain_col = jnp.sum(jnp.where(twice, mid_gain[...], 0.0), 1, keepdims=True)
    w_twice = dot(wo[...], one_hot(twice), 0, 1)
    even = (iota((chans, 2 * hidden), 1) & 1) == 0
    w_out = jnp.concatenate(
        [jnp.where(even, w_twice, 0.0), jnp.where(even, 0.0, w_twice)], 0
    ).astype(BF16)
    gain_all = jnp.broadcast_to(gain_col, (2 * hidden, b))

    pltpu.make_async_copy(q, q, sem_c_recv).wait()

    def total(v):
        t = jnp.sum(v.reshape(2 * hidden // 8, 8, b), 0)
        t = t + pltpu.roll(t, 4, 0)
        t = t + pltpu.roll(t, 2, 0)
        return jnp.broadcast_to(t[None], (2 * hidden // 8, 8, b)).reshape(2 * hidden, b)

    next_c = to_column(next_gain[...])

    def finish(j, ib, update):
        span = slice(ib * b, (ib + 1) * b)
        new = (pair_buf[j, :, span] + gate_buf[j, :, span] * update).astype(BF16)
        values = new.astype(F32)
        normed = normalize(values, next_c, 0)
        second = c == 1
        out_pair[j, :, span] = jnp.where(second, values[half:], values[:half]).astype(BF16)
        out_norm[j, :, span] = jnp.where(second, normed[half:], normed[:half]).astype(BF16)

    for w in range(5):
        t = q[w].reshape(2 * hidden, b).astype(F32)
        centred = t - total(t) * (1.0 / hidden)
        var = total(centred * centred) * (1.0 / hidden)
        tri = (centred * lax.rsqrt(var + EPS) * gain_all).astype(BF16)
        update = dot(w_out, tri, 1, 0)
        if w < 3:
            finish(0, w, update[:chans])
            finish(1, w, update[chans:])
        elif w == 3:
            finish(2, 0, update[:chans])
            finish(2, 1, update[chans:])
        else:
            finish(2, 2, update[:chans])

    part = sa.at[0 : k_n - 1]
    pltpu.make_async_copy(part, part, sem_a_send).wait()
    part = d.at[core]
    pltpu.make_async_copy(part, part, sem_f_send).wait()
    part = ps.at[:, 0 : r_n - 1]
    pltpu.make_async_copy(part, part, sem_p_send).wait()
    part = sc.at[:, 0 : k_n - 1]
    pltpu.make_async_copy(part, part, sem_c_send.at[0]).wait()
    pltpu.make_async_copy(sc, sc, sem_c_send.at[1]).wait()


def local(
    r_n,
    pair_rep,
    res_mask,
    in_gain,
    w_left,
    w_left_gate,
    w_right,
    w_right_gate,
    w_gate,
    mid_gain,
    w_out,
    next_gain,
):
    rows, n, chans = pair_rep.shape
    k_n = r_n // 2
    half = chans // 2
    vmem = pl.BlockSpec(memory_space=pltpu.VMEM)
    smem = pl.BlockSpec(memory_space=pltpu.SMEM)
    dma = pltpu.SemaphoreType.DMA
    out = jax.ShapeDtypeStruct((3, half, n), BF16)
    new_pair, new_norm = pl.pallas_call(
        functools.partial(kernel, r_n),
        out_shape=(out, out),
        in_specs=[vmem, smem] + [vmem] * 10,
        out_specs=(vmem, vmem),
        scratch_shapes=[
            pltpu.VMEM((k_n, 3, 3, 2, r_n), BF16),
            pltpu.VMEM((2, 3, k_n, 3, 2, r_n), BF16),
            pltpu.VMEM((5, r_n, 2, chans), BF16),
            pltpu.VMEM((5, r_n, 2, chans), BF16),
            pltpu.VMEM((5, k_n, 2, r_n), BF16),
            pltpu.VMEM((5, r_n, 2, r_n), BF16),
            pltpu.VMEM((3, chans, n), F32),
            pltpu.VMEM((3, chans, n), F32),
            dma,
            dma((GROUPS,)),
            dma,
            dma((GROUPS,)),
            dma,
            dma,
            dma((2,)),
            dma,
        ],
        compiler_params=pltpu.CompilerParams(collective_id=0, has_side_effects=True),
    )(
        pair_rep.reshape(rows * n, chans),
        res_mask,
        res_mask,
        in_gain.reshape(1, chans),
        w_left.T,
        w_left_gate.T,
        w_right.T,
        w_right_gate.T,
        w_gate,
        mid_gain.reshape(1, -1),
        w_out,
        next_gain.reshape(1, chans),
    )
    return jnp.transpose(new_pair, (2, 0, 1)), jnp.transpose(new_norm, (2, 0, 1))


def solution(mesh):
    return jax.shard_map(
        functools.partial(local, mesh.shape["row"]),
        mesh=mesh,
        in_specs=(
            P("row", None, None),
            P(),
            P(),
            P(None, "ch"),
            P(None, "ch"),
            P(None, "ch"),
            P(None, "ch"),
            P(),
            P(),
            P(),
            P(),
        ),
        out_specs=(P(None, "row", "ch"), P(None, "row", "ch")),
        check_vma=False,
    )
```

```python
import functools

import jax
import jax.numpy as jnp
from jax import lax
from jax.experimental import pallas as pl
from jax.experimental.pallas import tpu as pltpu
from jax.sharding import PartitionSpec as P

EPS = 1e-05
F32 = jnp.float32
BF16 = jnp.bfloat16
GROUPS = 4


def dot(a, b, ca, cb):
    return lax.dot_general(a, b, (((ca,), (cb,)), ((), ())), preferred_element_type=F32)


def iota(shape, dim):
    return lax.broadcasted_iota(jnp.int32, shape, dim)


def one_hot(cond):
    return jnp.where(cond, 1.0, 0.0).astype(BF16)


def to_column(row):
    size = row.shape[1]
    diagonal = iota((size, size), 0) == iota((size, size), 1)
    return jnp.sum(jnp.where(diagonal, row, 0.0), 1, keepdims=True)


def normalize(v, gain, along):
    scale = 1.0 / v.shape[along]
    centred = v - jnp.sum(v, along, keepdims=True) * scale
    var = jnp.sum(centred * centred, along, keepdims=True) * scale
    return centred * lax.rsqrt(var + EPS) * gain


def kernel(
    rows_n,
    x_any,
    mask_any,
    in_any,
    wl_any,
    wlg_any,
    wr_any,
    wrg_any,
    wg_any,
    mid_any,
    wo_any,
    next_any,
    out_pair,
    out_norm,
    x_ref,
    mask_smem,
    mask_row,
    in_gain,
    wl,
    wlg,
    wr,
    wrg,
    wg,
    mid_gain,
    wo,
    next_gain,
    sa,
    d,
    ps,
    pb,
    sc,
    q,
    gate_buf,
    pair_buf,
    sem_in,
    sem_known,
    sem_a_send,
    sem_a_recv,
    sem_f_send,
    sem_f_recv,
    sem_p_send,
    sem_p_recv,
    sem_c_send,
    sem_c_recv,
):
    r_n = rows_n
    k_n = r_n // 2
    n = 3 * r_n
    b = r_n
    chans = x_ref.shape[1]
    half = chans // 2
    me = lax.axis_index("row")
    c = lax.axis_index("ch")
    core = lax.rem(me, 2)
    slot = me // 2
    per = k_n // GROUPS
    x_n = 4 if r_n >= 128 else 2
    z_n = k_n // (2 * x_n)
    at_x = lax.rem(slot, x_n)
    at_y = lax.rem(slot // x_n, 2)
    at_z = slot // (2 * x_n)

    def chip(u, dy, dx):
        step = (u + 1) // 2
        ahead = lax.rem(u + core, 2) == 1
        z = lax.rem(at_z + jnp.where(ahead, step, z_n - step), z_n)
        return (z * 2 + lax.rem(at_y + dy, 2)) * x_n + lax.rem(at_x + dx, x_n)

    def tell(sem, u, dy, dx):
        target = {"row": 2 * chip(u, dy, dx) + core, "ch": c}
        pl.semaphore_signal(sem, inc=1, device_id=target)

    barrier = pltpu.get_barrier_semaphore()
    other_core = {"row": 2 * slot + 1 - core, "ch": c}
    other_ch = {"row": me, "ch": 1 - c}
    for t in range(1, z_n):
        tell(barrier, z_n - t, 0, 0)
    for t in range(1, x_n):
        tell(barrier, 0, 0, t)
    tell(barrier, 0, 1, 0)
    pl.semaphore_signal(barrier, inc=1, device_id=other_core)
    pl.semaphore_signal(barrier, inc=1, device_id=other_ch)

    arrays = (
        (x_any, x_ref),
        (wl_any, wl),
        (wlg_any, wlg),
        (wr_any, wr),
        (wrg_any, wrg),
        (in_any, in_gain),
        (mask_any, mask_smem),
        (mask_any, mask_row),
        (wg_any, wg),
        (mid_any, mid_gain),
        (wo_any, wo),
        (next_any, next_gain),
    )
    copies = [
        pltpu.make_async_copy(src, dst, sem_in.at[i]) for i, (src, dst) in enumerate(arrays)
    ]
    for copy in copies:
        copy.start()
    for copy in copies[:8]:
        copy.wait()

    hl = wl.shape[0]
    p_row, p_col = iota((2 * hl, hl), 0), iota((2 * hl, hl), 1)
    to_left, to_right = one_hot(p_row == 2 * p_col), one_hot(p_row == 2 * p_col + 1)
    w_lin = (dot(to_left, wl[...], 1, 0) + dot(to_right, wr[...], 1, 0)).astype(BF16)
    w_switch = (dot(to_left, wlg[...], 1, 0) + dot(to_right, wrg[...], 1, 0)).astype(BF16)
    group = slot // per

    def project(i):
        normed = normalize(x_ref[i * n : (i + 1) * n].astype(F32), in_gain[...], 1).astype(BF16)
        lin = dot(w_lin, normed, 1, 1)
        switch = dot(w_switch, normed, 1, 1)
        mask = mask_row[...].reshape(1, n).astype(F32) * mask_smem[3 * me + i].astype(F32)
        sides = (jax.nn.sigmoid(switch) * lin * mask).astype(BF16)
        for lb in range(3):
            sa[:, lb, i] = sides[:, lb * b : (lb + 1) * b].reshape(hl, 2, b)

    project(0)
    project(1)
    pl.semaphore_wait(barrier, z_n - 1 + x_n - 1 + 3)
    for t in range(1, x_n):
        tell(sem_known.at[0], 0, 0, t)
    project(2)
    pl.semaphore_wait(sem_known.at[0], x_n - 1)
    tell(sem_known.at[1], 0, 1, 0)

    group = slot // per

    def send_a(u, dy, dx):
        s = chip(u, dy, dx)
        pltpu.make_async_remote_copy(
            src_ref=sa.at[s],
            dst_ref=d.at[core, :, slot],
            send_sem=sem_a_send,
            recv_sem=sem_a_recv.at[group],
            device_id={"row": 2 * s + core, "ch": c},
        ).start()

    def near(t, carry):
        send_a(lax.rem(t, z_n), 0, t // z_n)
        return carry

    def far(t, carry):
        send_a(lax.rem(t, z_n), 1, t // z_n)
        return carry

    lax.fori_loop(1, z_n * x_n, near, 0)
    pl.semaphore_wait(sem_known.at[1], 1)
    pl.semaphore_signal(sem_known.at[2], inc=1, device_id=other_core)
    pl.semaphore_signal(sem_known.at[3], inc=1, device_id=other_ch)
    lax.fori_loop(0, z_n * x_n, far, 0)
    pltpu.make_async_copy(sa.at[slot], d.at[core, :, slot], sem_a_recv.at[group]).start()

    p_row, p_col = iota((2 * r_n, 2 * n), 0), iota((2 * r_n, 2 * n), 1)
    first = (p_row & 1) * n + 3 * (p_row >> 1)
    for j in range(3):
        rows = dot(one_hot(p_col == first + j), x_ref[0 : 2 * n], 1, 0)
        ps[j] = rows.astype(BF16).reshape(r_n, 2, chans)
    p_row, p_col = iota((2 * r_n, n), 0), iota((2 * r_n, n), 1)
    last = x_ref[2 * n : 3 * n]
    rows = dot(one_hot(p_col == 3 * (p_row >> 1) + (p_row & 1)), last, 1, 0)
    ps[3] = rows.astype(BF16).reshape(r_n, 2, chans)
    rows = dot(one_hot(p_col == 3 * (p_row >> 1) + 2), last, 1, 0)
    ps[4] = rows.astype(BF16).reshape(r_n, 2, chans)

    def send_p(to_core):
        def send(t, carry):
            s = chip(lax.rem(t, z_n), t // (z_n * x_n), lax.rem(t // z_n, x_n))
            r = 2 * s + to_core
            pltpu.make_async_remote_copy(
                src_ref=ps.at[:, r],
                dst_ref=pb.at[:, me],
                send_sem=sem_p_send,
                recv_sem=sem_p_recv,
                device_id={"row": r, "ch": c},
            ).start()
            return carry

        return send

    pl.semaphore_wait(sem_known.at[2], 1)
    lax.fori_loop(1, k_n, send_p(core), 0)
    lax.fori_loop(0, k_n, send_p(1 - core), 0)
    pltpu.make_async_copy(ps.at[:, me], pb.at[:, me], sem_p_recv).start()

    s_row, s_col = iota((n, n), 0), iota((n, n), 1)
    sixth = (s_col * 10923) >> 16
    left_at = 6 * sixth + ((s_col - 6 * sixth) >> 1)
    is_left = (s_col & 1) == 0
    sel_left = [one_hot((s_row == left_at + 3 * h) & is_left) for h in range(2)]
    s_row, s_col = iota((2 * r_n, n), 0), iota((2 * r_n, n), 1)
    in_two = s_row < r_n
    s_two = jnp.where(in_two, s_row, s_row - r_n)
    sel_right = one_hot(
        s_col == 6 * (s_two >> 1) + jnp.where(in_two, 2 * (s_two & 1) + 1, 5)
    )

    for g in range(GROUPS):
        part = d.at[core, :, g * per : (g + 1) * per]
        pltpu.make_async_copy(part, part, sem_a_recv.at[g]).wait()
        pltpu.make_async_remote_copy(
            src_ref=part,
            dst_ref=part,
            send_sem=sem_f_send,
            recv_sem=sem_f_recv.at[g],
            device_id=other_core,
        ).start()
    for g in range(GROUPS):
        part = d.at[1 - core, :, g * per : (g + 1) * per]
        pltpu.make_async_copy(part, part, sem_f_recv.at[g]).wait()

    lefts, rights = [], []
    for lb in range(3):
        acc = dot(sel_left[0], d[0, lb].reshape(2 * n // 2, b), 1, 0)
        acc = acc + dot(sel_left[1], d[1, lb].reshape(2 * n // 2, b), 1, 0)
        lefts.append(acc.astype(BF16))
        rights.append(dot(sel_right, d[core, lb].reshape(n, b), 1, 0).astype(BF16))
    triangle = dot(jnp.concatenate(rights, 1), jnp.concatenate(lefts, 1), 1, 1)
    upper, lower = triangle[:r_n], triangle[r_n:]
    for ib in range(3):
        sc[ib] = upper[:, ib * b : (ib + 1) * b].astype(BF16).reshape(k_n, 2, b)
    odd = (iota((r_n, b), 0) & 1) == 1
    sc[3] = jnp.where(odd, lower[:, b : 2 * b], lower[:, :b]).astype(BF16).reshape(k_n, 2, b)
    sc[4] = lower[:, 2 * b :].astype(BF16).reshape(k_n, 2, b)

    k_me = c * k_n + slot

    def send_c(index, to_ch):
        def send(t, carry):
            s = chip(lax.rem(t, z_n), t // (z_n * x_n), lax.rem(t // z_n, x_n))
            pltpu.make_async_remote_copy(
                src_ref=sc.at[:, s],
                dst_ref=q.at[:, k_me],
                send_sem=sem_c_send.at[index],
                recv_sem=sem_c_recv,
                device_id={"row": 2 * s + core, "ch": to_ch},
            ).start()
            return carry

        return send

    pl.semaphore_wait(sem_known.at[3], 1)
    lax.fori_loop(0, k_n, send_c(1, 1 - c), 0)
    lax.fori_loop(1, k_n, send_c(0, c), 0)
    pltpu.make_async_copy(sc.at[:, slot], q.at[:, k_me], sem_c_recv).start()

    for copy in copies[8:]:
        copy.wait()
    pltpu.make_async_copy(pb, pb, sem_p_recv).wait()
    s_row, s_col = iota((2 * r_n, n), 0), iota((2 * r_n, n), 1)
    sel_two = one_hot(s_col == 3 * (s_row >> 1) + (s_row & 1))
    third = s_col == 3 * (s_row >> 1) + 2
    sel_last = [one_hot(third & ((s_row & 1) == s)) for s in range(2)]
    gain_c = to_column(in_gain[...])
    for j in range(3):
        rest = pb[3 + j // 2].reshape(2 * r_n, chans)
        cells = dot(pb[j].reshape(2 * r_n, chans), sel_two, 0, 0) + dot(rest, sel_last[j % 2], 0, 0)
        pair_buf[j] = cells
        normed = normalize(cells, gain_c, 0).astype(BF16)
        gate_buf[j] = jax.nn.sigmoid(dot(wg[...], normed, 0, 0))

    hidden = wo.shape[0]
    p_row, p_col = iota((2 * hidden, hidden), 0), iota((2 * hidden, hidden), 1)
    twice = (p_row >> 1) == p_col
    gain_col = jnp.sum(jnp.where(twice, mid_gain[...], 0.0), 1, keepdims=True)
    w_twice = dot(wo[...], one_hot(twice), 0, 1)
    even = (iota((chans, 2 * hidden), 1) & 1) == 0
    w_out = jnp.concatenate(
        [jnp.where(even, w_twice, 0.0), jnp.where(even, 0.0, w_twice)], 0
    ).astype(BF16)
    gain_all = jnp.broadcast_to(gain_col, (2 * hidden, b))

    pltpu.make_async_copy(q, q, sem_c_recv).wait()

    def total(v):
        t = jnp.sum(v.reshape(2 * hidden // 8, 8, b), 0)
        t = t + pltpu.roll(t, 4, 0)
        t = t + pltpu.roll(t, 2, 0)
        return jnp.broadcast_to(t[None], (2 * hidden // 8, 8, b)).reshape(2 * hidden, b)

    next_c = to_column(next_gain[...])

    def finish(j, ib, update):
        span = slice(ib * b, (ib + 1) * b)
        new = (pair_buf[j, :, span] + gate_buf[j, :, span] * update).astype(BF16)
        values = new.astype(F32)
        normed = normalize(values, next_c, 0)
        second = c == 1
        out_pair[j, :, span] = jnp.where(second, values[half:], values[:half]).astype(BF16)
        out_norm[j, :, span] = jnp.where(second, normed[half:], normed[:half]).astype(BF16)

    for w in range(5):
        t = q[w].reshape(2 * hidden, b).astype(F32)
        centred = t - total(t) * (1.0 / hidden)
        var = total(centred * centred) * (1.0 / hidden)
        tri = (centred * lax.rsqrt(var + EPS) * gain_all).astype(BF16)
        update = dot(w_out, tri, 1, 0)
        if w < 3:
            finish(0, w, update[:chans])
            finish(1, w, update[chans:])
        elif w == 3:
            finish(2, 0, update[:chans])
            finish(2, 1, update[chans:])
        else:
            finish(2, 2, update[:chans])

    part = sa.at[0 : k_n - 1]
    pltpu.make_async_copy(part, part, sem_a_send).wait()
    part = d.at[core]
    pltpu.make_async_copy(part, part, sem_f_send).wait()
    part = ps.at[:, 0 : r_n - 1]
    pltpu.make_async_copy(part, part, sem_p_send).wait()
    part = sc.at[:, 0 : k_n - 1]
    pltpu.make_async_copy(part, part, sem_c_send.at[0]).wait()
    pltpu.make_async_copy(sc, sc, sem_c_send.at[1]).wait()


def local(
    r_n,
    pair_rep,
    res_mask,
    in_gain,
    w_left,
    w_left_gate,
    w_right,
    w_right_gate,
    w_gate,
    mid_gain,
    w_out,
    next_gain,
):
    rows, n, chans = pair_rep.shape
    k_n = r_n // 2
    half = chans // 2
    hl = w_left.shape[1]
    vmem = pl.BlockSpec(memory_space=pltpu.VMEM)
    place = pl.BlockSpec(memory_space=pl.ANY)
    dma = pltpu.SemaphoreType.DMA
    out = jax.ShapeDtypeStruct((3, half, n), BF16)
    new_pair, new_norm = pl.pallas_call(
        functools.partial(kernel, r_n),
        out_shape=(out, out),
        in_specs=[place] * 11,
        out_specs=(vmem, vmem),
        scratch_shapes=[
            pltpu.VMEM((rows * n, chans), BF16),
            pltpu.SMEM((n,), jnp.int32),
            pltpu.VMEM((n,), jnp.int32),
            pltpu.VMEM((1, chans), F32),
            pltpu.VMEM((hl, chans), BF16),
            pltpu.VMEM((hl, chans), BF16),
            pltpu.VMEM((hl, chans), BF16),
            pltpu.VMEM((hl, chans), BF16),
            pltpu.VMEM((chans, chans), BF16),
            pltpu.VMEM((1, r_n), F32),
            pltpu.VMEM((r_n, chans), BF16),
            pltpu.VMEM((1, chans), F32),
            pltpu.VMEM((k_n, 3, 3, 2, r_n), BF16),
            pltpu.VMEM((2, 3, k_n, 3, 2, r_n), BF16),
            pltpu.VMEM((5, r_n, 2, chans), BF16),
            pltpu.VMEM((5, r_n, 2, chans), BF16),
            pltpu.VMEM((5, k_n, 2, r_n), BF16),
            pltpu.VMEM((5, r_n, 2, r_n), BF16),
            pltpu.VMEM((3, chans, n), F32),
            pltpu.VMEM((3, chans, n), F32),
            dma((12,)),
            pltpu.SemaphoreType.REGULAR((4,)),
            dma,
            dma((GROUPS,)),
            dma,
            dma((GROUPS,)),
            dma,
            dma,
            dma((2,)),
            dma,
        ],
        compiler_params=pltpu.CompilerParams(collective_id=0, has_side_effects=True),
    )(
        pair_rep.reshape(rows * n, chans),
        res_mask,
        in_gain.reshape(1, chans),
        w_left.T,
        w_left_gate.T,
        w_right.T,
        w_right_gate.T,
        w_gate,
        mid_gain.reshape(1, -1),
        w_out,
        next_gain.reshape(1, chans),
    )
    return jnp.transpose(new_pair, (2, 0, 1)), jnp.transpose(new_norm, (2, 0, 1))


def solution(mesh):
    return jax.shard_map(
        functools.partial(local, mesh.shape["row"]),
        mesh=mesh,
        in_specs=(
            P("row", None, None),
            P(),
            P(),
            P(None, "ch"),
            P(None, "ch"),
            P(None, "ch"),
            P(None, "ch"),
            P(),
            P(),
            P(),
            P(),
        ),
        out_specs=(P(None, "row", "ch"), P(None, "row", "ch")),
        check_vma=False,
    )
```

```python
import functools

import jax
import jax.numpy as jnp
from jax import lax
from jax.experimental import pallas as pl
from jax.experimental.pallas import tpu as pltpu
from jax.sharding import PartitionSpec as P

EPS = 1e-05
F32 = jnp.float32
BF16 = jnp.bfloat16
GROUPS = 4


def dot(a, b, ca, cb):
    return lax.dot_general(a, b, (((ca,), (cb,)), ((), ())), preferred_element_type=F32)


def iota(shape, dim):
    return lax.broadcasted_iota(jnp.int32, shape, dim)


def one_hot(cond):
    return jnp.where(cond, 1.0, 0.0).astype(BF16)


def to_column(row):
    size = row.shape[1]
    diagonal = iota((size, size), 0) == iota((size, size), 1)
    return jnp.sum(jnp.where(diagonal, row, 0.0), 1, keepdims=True)


def normalize(v, gain, along):
    scale = 1.0 / v.shape[along]
    centred = v - jnp.sum(v, along, keepdims=True) * scale
    var = jnp.sum(centred * centred, along, keepdims=True) * scale
    return centred * lax.rsqrt(var + EPS) * gain


def kernel(
    rows_n,
    x_any,
    mask_any,
    in_any,
    wl_any,
    wlg_any,
    wr_any,
    wrg_any,
    wg_any,
    mid_any,
    wo_any,
    next_any,
    out_pair,
    out_norm,
    x_ref,
    mask_smem,
    mask_row,
    in_gain,
    wl,
    wlg,
    wr,
    wrg,
    wg,
    mid_gain,
    wo,
    next_gain,
    sa,
    d,
    ps,
    pb,
    sc,
    q,
    gate_buf,
    pair_buf,
    sem_in,
    sem_known,
    sem_a_send,
    sem_a_recv,
    sem_f_send,
    sem_f_recv,
    sem_p_send,
    sem_p_recv,
    sem_c_send,
    sem_c_recv,
):
    r_n = rows_n
    k_n = r_n // 2
    n = 3 * r_n
    b = r_n
    chans = x_ref.shape[1]
    half = chans // 2
    me = lax.axis_index("row")
    c = lax.axis_index("ch")
    core = lax.rem(me, 2)
    slot = me // 2
    per = k_n // GROUPS
    x_n = 4 if r_n >= 128 else 2
    z_n = k_n // (2 * x_n)
    at_x = lax.rem(slot, x_n)
    at_y = lax.rem(slot // x_n, 2)
    at_z = slot // (2 * x_n)

    ahead = 1 - 2 * core
    planes = [
        lax.rem(at_z + z_n + ((u + 1) // 2) * (ahead if u % 2 else -ahead), z_n) * (2 * x_n)
        for u in range(z_n)
    ]

    def column(dy, dx):
        return lax.rem(at_y + dy, 2) * x_n + lax.rem(at_x + dx, x_n)

    here = column(0, 0)

    def tell(sem, chip):
        pl.semaphore_signal(sem, inc=1, device_id={"row": 2 * chip + core, "ch": c})

    def tell_row(sem):
        for t in range(1, x_n):
            tell(sem, planes[0] + column(0, t))

    def all_chips(send, dy, last):
        def some(t, carry):
            to = column(dy, x_n - 1 - t)
            for u in reversed(range(z_n)):
                send(planes[u] + to)
            return carry

        lax.fori_loop(0, x_n - 1, some, 0)
        for u in reversed(range(last, z_n)):
            send(planes[u] + column(dy, 0))

    barrier = pltpu.get_barrier_semaphore()
    other_core = {"row": 2 * slot + 1 - core, "ch": c}
    other_ch = {"row": me, "ch": 1 - c}
    for u in reversed(range(1, z_n)):
        tell(barrier, planes[u] + here)
    tell_row(barrier)
    tell(barrier, planes[0] + column(1, 0))
    pl.semaphore_signal(barrier, inc=1, device_id=other_core)
    pl.semaphore_signal(barrier, inc=1, device_id=other_ch)

    arrays = (
        (x_any, x_ref),
        (wl_any, wl),
        (wlg_any, wlg),
        (wr_any, wr),
        (wrg_any, wrg),
        (in_any, in_gain),
        (mask_any, mask_smem),
        (mask_any, mask_row),
        (wg_any, wg),
        (mid_any, mid_gain),
        (wo_any, wo),
        (next_any, next_gain),
    )
    copies = [
        pltpu.make_async_copy(src, dst, sem_in.at[i]) for i, (src, dst) in enumerate(arrays)
    ]
    for copy in copies:
        copy.start()
    for copy in copies[:8]:
        copy.wait()

    hl = wl.shape[0]
    p_row, p_col = iota((2 * hl, hl), 0), iota((2 * hl, hl), 1)
    to_left, to_right = one_hot(p_row == 2 * p_col), one_hot(p_row == 2 * p_col + 1)
    w_lin = (dot(to_left, wl[...], 1, 0) + dot(to_right, wr[...], 1, 0)).astype(BF16)
    w_switch = (dot(to_left, wlg[...], 1, 0) + dot(to_right, wrg[...], 1, 0)).astype(BF16)
    group = slot // per

    def project(i):
        normed = normalize(x_ref[i * n : (i + 1) * n].astype(F32), in_gain[...], 1).astype(BF16)
        lin = dot(w_lin, normed, 1, 1)
        switch = dot(w_switch, normed, 1, 1)
        mask = mask_row[...].reshape(1, n).astype(F32) * mask_smem[3 * me + i].astype(F32)
        sides = (jax.nn.sigmoid(switch) * lin * mask).astype(BF16)
        for lb in range(3):
            sa[:, lb, i] = sides[:, lb * b : (lb + 1) * b].reshape(hl, 2, b)

    project(0)
    project(1)
    pl.semaphore_wait(barrier, z_n - 1 + x_n - 1 + 3)
    tell_row(sem_known.at[0])
    project(2)

    def send_a(s):
        pltpu.make_async_remote_copy(
            src_ref=sa.at[s],
            dst_ref=d.at[core, :, slot],
            send_sem=sem_a_send,
            recv_sem=sem_a_recv.at[group],
            device_id={"row": 2 * s + core, "ch": c},
        ).start()

    for u in reversed(range(1, z_n)):
        send_a(planes[u] + here)
    pl.semaphore_wait(sem_known.at[0], x_n - 1)
    tell(sem_known.at[1], planes[0] + column(1, 0))

    all_chips(send_a, 0, z_n)
    pl.semaphore_wait(sem_known.at[1], 1)
    pl.semaphore_signal(sem_known.at[2], inc=1, device_id=other_core)
    pl.semaphore_signal(sem_known.at[3], inc=1, device_id=other_ch)
    all_chips(send_a, 1, 0)
    pltpu.make_async_copy(sa.at[slot], d.at[core, :, slot], sem_a_recv.at[group]).start()

    p_row, p_col = iota((2 * r_n, 2 * n), 0), iota((2 * r_n, 2 * n), 1)
    first = (p_row & 1) * n + 3 * (p_row >> 1)
    for j in range(3):
        rows = dot(one_hot(p_col == first + j), x_ref[0 : 2 * n], 1, 0)
        ps[j] = rows.astype(BF16).reshape(r_n, 2, chans)
    p_row, p_col = iota((2 * r_n, n), 0), iota((2 * r_n, n), 1)
    last = x_ref[2 * n : 3 * n]
    rows = dot(one_hot(p_col == 3 * (p_row >> 1) + (p_row & 1)), last, 1, 0)
    ps[3] = rows.astype(BF16).reshape(r_n, 2, chans)
    rows = dot(one_hot(p_col == 3 * (p_row >> 1) + 2), last, 1, 0)
    ps[4] = rows.astype(BF16).reshape(r_n, 2, chans)

    def send_p(to_core):
        def send(s):
            r = 2 * s + to_core
            pltpu.make_async_remote_copy(
                src_ref=ps.at[:, r],
                dst_ref=pb.at[:, me],
                send_sem=sem_p_send,
                recv_sem=sem_p_recv,
                device_id={"row": r, "ch": c},
            ).start()

        return send

    pl.semaphore_wait(sem_known.at[2], 1)
    all_chips(send_p(core), 1, 0)
    all_chips(send_p(1 - core), 1, 0)
    all_chips(send_p(core), 0, 1)
    all_chips(send_p(1 - core), 0, 0)
    pltpu.make_async_copy(ps.at[:, me], pb.at[:, me], sem_p_recv).start()

    s_row, s_col = iota((n, n), 0), iota((n, n), 1)
    sixth = (s_col * 10923) >> 16
    left_at = 6 * sixth + ((s_col - 6 * sixth) >> 1)
    is_left = (s_col & 1) == 0
    sel_own = one_hot((s_row == left_at + 3 * core) & is_left)
    sel_other = one_hot((s_row == left_at + 3 * (1 - core)) & is_left)
    s_row, s_col = iota((2 * r_n, n), 0), iota((2 * r_n, n), 1)
    in_two = s_row < r_n
    s_two = jnp.where(in_two, s_row, s_row - r_n)
    sel_right = one_hot(
        s_col == 6 * (s_two >> 1) + jnp.where(in_two, 2 * (s_two & 1) + 1, 5)
    )

    for g in range(GROUPS):
        part = d.at[core, :, g * per : (g + 1) * per]
        pltpu.make_async_copy(part, part, sem_a_recv.at[g]).wait()
        pltpu.make_async_remote_copy(
            src_ref=part,
            dst_ref=part,
            send_sem=sem_f_send,
            recv_sem=sem_f_recv.at[g],
            device_id=other_core,
        ).start()

    owns = [d[core, lb].reshape(n, b) for lb in range(3)]
    own_left = [dot(sel_own, own, 1, 0) for own in owns]
    right = jnp.concatenate([dot(sel_right, own, 1, 0).astype(BF16) for own in owns], 1)
    for g in range(GROUPS):
        part = d.at[1 - core, :, g * per : (g + 1) * per]
        pltpu.make_async_copy(part, part, sem_f_recv.at[g]).wait()
    lefts = []
    for lb in range(3):
        acc = own_left[lb] + dot(sel_other, d[1 - core, lb].reshape(n, b), 1, 0)
        lefts.append(acc.astype(BF16))
    triangle = dot(right, jnp.concatenate(lefts, 1), 1, 1)
    upper, lower = triangle[:r_n], triangle[r_n:]
    for ib in range(3):
        sc[ib] = upper[:, ib * b : (ib + 1) * b].astype(BF16).reshape(k_n, 2, b)
    odd = (iota((r_n, b), 0) & 1) == 1
    sc[3] = jnp.where(odd, lower[:, b : 2 * b], lower[:, :b]).astype(BF16).reshape(k_n, 2, b)
    sc[4] = lower[:, 2 * b :].astype(BF16).reshape(k_n, 2, b)

    k_me = c * k_n + slot

    def send_c(index, to_ch):
        def send(s):
            pltpu.make_async_remote_copy(
                src_ref=sc.at[:, s],
                dst_ref=q.at[:, k_me],
                send_sem=sem_c_send.at[index],
                recv_sem=sem_c_recv,
                device_id={"row": 2 * s + core, "ch": to_ch},
            ).start()

        return send

    pl.semaphore_wait(sem_known.at[3], 1)
    all_chips(send_c(1, 1 - c), 1, 0)
    all_chips(send_c(1, 1 - c), 0, 0)
    all_chips(send_c(0, c), 1, 0)
    all_chips(send_c(0, c), 0, 1)
    pltpu.make_async_copy(sc.at[:, slot], q.at[:, k_me], sem_c_recv).start()

    for copy in copies[8:]:
        copy.wait()
    pltpu.make_async_copy(pb, pb, sem_p_recv).wait()
    s_row, s_col = iota((2 * r_n, n), 0), iota((2 * r_n, n), 1)
    sel_two = one_hot(s_col == 3 * (s_row >> 1) + (s_row & 1))
    third = s_col == 3 * (s_row >> 1) + 2
    sel_last = [one_hot(third & ((s_row & 1) == s)) for s in range(2)]
    gain_c = to_column(in_gain[...])
    for j in range(3):
        rest = pb[3 + j // 2].reshape(2 * r_n, chans)
        cells = dot(pb[j].reshape(2 * r_n, chans), sel_two, 0, 0) + dot(rest, sel_last[j % 2], 0, 0)
        pair_buf[j] = cells
        normed = normalize(cells, gain_c, 0).astype(BF16)
        gate_buf[j] = jax.nn.sigmoid(dot(wg[...], normed, 0, 0))

    hidden = wo.shape[0]
    p_row, p_col = iota((2 * hidden, hidden), 0), iota((2 * hidden, hidden), 1)
    twice = (p_row >> 1) == p_col
    gain_col = jnp.sum(jnp.where(twice, mid_gain[...], 0.0), 1, keepdims=True)
    w_twice = dot(wo[...], one_hot(twice), 0, 1)
    even = (iota((chans, 2 * hidden), 1) & 1) == 0
    w_out = jnp.concatenate(
        [jnp.where(even, w_twice, 0.0), jnp.where(even, 0.0, w_twice)], 0
    ).astype(BF16)
    gain_all = jnp.broadcast_to(gain_col, (2 * hidden, b))

    pltpu.make_async_copy(q, q, sem_c_recv).wait()

    def total(v):
        t = jnp.sum(v.reshape(2 * hidden // 8, 8, b), 0)
        t = t + pltpu.roll(t, 4, 0)
        t = t + pltpu.roll(t, 2, 0)
        return jnp.broadcast_to(t[None], (2 * hidden // 8, 8, b)).reshape(2 * hidden, b)

    next_c = to_column(next_gain[...])

    def finish(j, ib, update):
        span = slice(ib * b, (ib + 1) * b)
        new = (pair_buf[j, :, span] + gate_buf[j, :, span] * update).astype(BF16)
        values = new.astype(F32)
        normed = normalize(values, next_c, 0)
        second = c == 1
        out_pair[j, :, span] = jnp.where(second, values[half:], values[:half]).astype(BF16)
        out_norm[j, :, span] = jnp.where(second, normed[half:], normed[:half]).astype(BF16)

    for w in range(5):
        t = q[w].reshape(2 * hidden, b).astype(F32)
        centred = t - total(t) * (1.0 / hidden)
        var = total(centred * centred) * (1.0 / hidden)
        tri = (centred * lax.rsqrt(var + EPS) * gain_all).astype(BF16)
        update = dot(w_out, tri, 1, 0)
        if w < 3:
            finish(0, w, update[:chans])
            finish(1, w, update[chans:])
        elif w == 3:
            finish(2, 0, update[:chans])
            finish(2, 1, update[chans:])
        else:
            finish(2, 2, update[:chans])

    part = sa.at[0 : k_n - 1]
    pltpu.make_async_copy(part, part, sem_a_send).wait()
    part = d.at[core]
    pltpu.make_async_copy(part, part, sem_f_send).wait()
    part = ps.at[:, 0 : r_n - 1]
    pltpu.make_async_copy(part, part, sem_p_send).wait()
    part = sc.at[:, 0 : k_n - 1]
    pltpu.make_async_copy(part, part, sem_c_send.at[0]).wait()
    pltpu.make_async_copy(sc, sc, sem_c_send.at[1]).wait()


def local(
    r_n,
    pair_rep,
    res_mask,
    in_gain,
    w_left,
    w_left_gate,
    w_right,
    w_right_gate,
    w_gate,
    mid_gain,
    w_out,
    next_gain,
):
    rows, n, chans = pair_rep.shape
    k_n = r_n // 2
    half = chans // 2
    hl = w_left.shape[1]
    vmem = pl.BlockSpec(memory_space=pltpu.VMEM)
    place = pl.BlockSpec(memory_space=pltpu.HBM)
    dma = pltpu.SemaphoreType.DMA
    out = jax.ShapeDtypeStruct((3, half, n), BF16)
    new_pair, new_norm = pl.pallas_call(
        functools.partial(kernel, r_n),
        out_shape=(out, out),
        in_specs=[place] * 11,
        out_specs=(vmem, vmem),
        scratch_shapes=[
            pltpu.VMEM((rows * n, chans), BF16),
            pltpu.SMEM((n,), jnp.int32),
            pltpu.VMEM((n,), jnp.int32),
            pltpu.VMEM((1, chans), F32),
            pltpu.VMEM((hl, chans), BF16),
            pltpu.VMEM((hl, chans), BF16),
            pltpu.VMEM((hl, chans), BF16),
            pltpu.VMEM((hl, chans), BF16),
            pltpu.VMEM((chans, chans), BF16),
            pltpu.VMEM((1, r_n), F32),
            pltpu.VMEM((r_n, chans), BF16),
            pltpu.VMEM((1, chans), F32),
            pltpu.VMEM((k_n, 3, 3, 2, r_n), BF16),
            pltpu.VMEM((2, 3, k_n, 3, 2, r_n), BF16),
            pltpu.VMEM((5, r_n, 2, chans), BF16),
            pltpu.VMEM((5, r_n, 2, chans), BF16),
            pltpu.VMEM((5, k_n, 2, r_n), BF16),
            pltpu.VMEM((5, r_n, 2, r_n), BF16),
            pltpu.VMEM((3, chans, n), F32),
            pltpu.VMEM((3, chans, n), F32),
            dma((12,)),
            pltpu.SemaphoreType.REGULAR((4,)),
            dma,
            dma((GROUPS,)),
            dma,
            dma((GROUPS,)),
            dma,
            dma,
            dma((2,)),
            dma,
        ],
        compiler_params=pltpu.CompilerParams(
            collective_id=0, has_side_effects=True, vmem_limit_bytes=8 * 1024 * 1024
        ),
    )(
        *(
            pltpu.with_memory_space_constraint(a, pltpu.HBM)
            for a in (
                pair_rep.reshape(rows * n, chans),
                res_mask,
                in_gain.reshape(1, chans),
                w_left.T,
                w_left_gate.T,
                w_right.T,
                w_right_gate.T,
                w_gate,
                mid_gain.reshape(1, -1),
                w_out,
                next_gain.reshape(1, chans),
            )
        )
    )
    return jnp.transpose(new_pair, (2, 0, 1)), jnp.transpose(new_norm, (2, 0, 1))


def solution(mesh):
    return jax.shard_map(
        functools.partial(local, mesh.shape["row"]),
        mesh=mesh,
        in_specs=(
            P("row", None, None),
            P(),
            P(),
            P(None, "ch"),
            P(None, "ch"),
            P(None, "ch"),
            P(None, "ch"),
            P(),
            P(),
            P(),
            P(),
        ),
        out_specs=(P(None, "row", "ch"), P(None, "row", "ch")),
        check_vma=False,
    )
```

```python
import functools

import jax
import jax.numpy as jnp
from jax import lax
from jax.experimental import pallas as pl
from jax.experimental.pallas import tpu as pltpu
from jax.sharding import PartitionSpec as P

EPS = 1e-05
F32 = jnp.float32
BF16 = jnp.bfloat16
GROUPS = 4


def dot(a, b, ca, cb):
    return lax.dot_general(a, b, (((ca,), (cb,)), ((), ())), preferred_element_type=F32)


def iota(shape, dim):
    return lax.broadcasted_iota(jnp.int32, shape, dim)


def one_hot(cond):
    return jnp.where(cond, 1.0, 0.0).astype(BF16)


def to_column(row):
    size = row.shape[1]
    diagonal = iota((size, size), 0) == iota((size, size), 1)
    return jnp.sum(jnp.where(diagonal, row, 0.0), 1, keepdims=True)


def normalize(v, gain, along):
    scale = 1.0 / v.shape[along]
    centred = v - jnp.sum(v, along, keepdims=True) * scale
    var = jnp.sum(centred * centred, along, keepdims=True) * scale
    return centred * lax.rsqrt(var + EPS) * gain


def kernel(
    rows_n,
    x_any,
    mask_any,
    in_any,
    wl_any,
    wlg_any,
    wr_any,
    wrg_any,
    wg_any,
    mid_any,
    wo_any,
    next_any,
    out_pair,
    out_norm,
    x_ref,
    mask_smem,
    mask_row,
    in_gain,
    wl,
    wlg,
    wr,
    wrg,
    wg,
    mid_gain,
    wo,
    next_gain,
    sa,
    d,
    ps,
    pb,
    sc,
    q,
    gate_buf,
    pair_buf,
    sem_in,
    sem_known,
    sem_a_send,
    sem_a_recv,
    sem_f_send,
    sem_f_recv,
    sem_p_send,
    sem_p_recv,
    sem_c_send,
    sem_c_recv,
):
    r_n = rows_n
    k_n = r_n // 2
    n = 3 * r_n
    b = r_n
    chans = x_ref.shape[1]
    half = chans // 2
    me = lax.axis_index("row")
    c = lax.axis_index("ch")
    core = lax.rem(me, 2)
    slot = me // 2
    per = k_n // GROUPS
    x_n = 4 if r_n >= 128 else 2
    z_n = k_n // (2 * x_n)
    at_x = lax.rem(slot, x_n)
    at_y = lax.rem(slot // x_n, 2)
    at_z = slot // (2 * x_n)

    ahead = 1 - 2 * core
    planes = [
        lax.rem(at_z + z_n + ((u + 1) // 2) * (ahead if u % 2 else -ahead), z_n) * (2 * x_n)
        for u in range(z_n)
    ]

    def column(dy, dx):
        return lax.rem(at_y + dy, 2) * x_n + lax.rem(at_x + dx, x_n)

    here = column(0, 0)

    def tell(sem, chip):
        pl.semaphore_signal(sem, inc=1, device_id={"row": 2 * chip + 1, "ch": c})

    def tell_row(sem):
        for t in range(1, x_n):
            tell(sem, planes[0] + column(0, t))

    def all_chips(send, dy, last):
        def some(t, carry):
            to = column(dy, x_n - 1 - t)
            for u in reversed(range(z_n)):
                send(planes[u] + to)
            return carry

        lax.fori_loop(0, x_n - 1, some, 0)
        for u in reversed(range(last, z_n)):
            send(planes[u] + column(dy, 0))

    barrier = pltpu.get_barrier_semaphore()
    other_core = {"row": 2 * slot + 1 - core, "ch": c}
    other_ch = {"row": me, "ch": 1 - c}

    def tell_other_core(sem):
        pl.semaphore_signal(sem, inc=1, device_id=other_core)

    for u in reversed(range(1, z_n)):
        tell(barrier, planes[u] + here)
    tell_row(barrier)
    tell(barrier, planes[0] + column(1, 0))

    @pl.when(core == 0)
    def _():
        tell_other_core(barrier)

    @pl.when(core == 1)
    def _():
        pl.semaphore_signal(barrier, inc=1, device_id=other_ch)

    arrays = (
        (x_any, x_ref),
        (wl_any, wl),
        (wlg_any, wlg),
        (wr_any, wr),
        (wrg_any, wrg),
        (in_any, in_gain),
        (mask_any, mask_smem),
        (mask_any, mask_row),
        (wg_any, wg),
        (mid_any, mid_gain),
        (wo_any, wo),
        (next_any, next_gain),
    )
    copies = [
        pltpu.make_async_copy(src, dst, sem_in.at[i]) for i, (src, dst) in enumerate(arrays)
    ]
    for copy in copies:
        copy.start()
    for copy in copies[:8]:
        copy.wait()

    hl = wl.shape[0]
    p_row, p_col = iota((2 * hl, hl), 0), iota((2 * hl, hl), 1)
    to_left, to_right = one_hot(p_row == 2 * p_col), one_hot(p_row == 2 * p_col + 1)
    w_lin = (dot(to_left, wl[...], 1, 0) + dot(to_right, wr[...], 1, 0)).astype(BF16)
    w_switch = (dot(to_left, wlg[...], 1, 0) + dot(to_right, wrg[...], 1, 0)).astype(BF16)
    group = slot // per

    def project(i):
        normed = normalize(x_ref[i * n : (i + 1) * n].astype(F32), in_gain[...], 1).astype(BF16)
        lin = dot(w_lin, normed, 1, 1)
        switch = dot(w_switch, normed, 1, 1)
        mask = mask_row[...].reshape(1, n).astype(F32) * mask_smem[3 * me + i].astype(F32)
        sides = (jax.nn.sigmoid(switch) * lin * mask).astype(BF16)
        for lb in range(3):
            sa[:, lb, i] = sides[:, lb * b : (lb + 1) * b].reshape(hl, 2, b)

    project(0)
    project(1)
    @pl.when(core == 1)
    def _():
        pl.semaphore_wait(barrier, 2 * (z_n + x_n - 1) + 2)
        tell_row(sem_known.at[0])
        tell_other_core(barrier)

    @pl.when(core == 0)
    def _():
        pl.semaphore_wait(barrier, 1)

    project(2)

    def send_a(s):
        pltpu.make_async_remote_copy(
            src_ref=sa.at[s],
            dst_ref=d.at[core, :, slot],
            send_sem=sem_a_send,
            recv_sem=sem_a_recv.at[group],
            device_id={"row": 2 * s + 1 - core, "ch": c},
        ).start()

    for u in reversed(range(1, z_n)):
        send_a(planes[u] + here)

    @pl.when(core == 1)
    def _():
        pl.semaphore_wait(sem_known.at[0], x_n - 1)
        tell(sem_known.at[1], planes[0] + column(1, 0))
        tell_other_core(sem_known.at[0])

    @pl.when(core == 0)
    def _():
        pl.semaphore_wait(sem_known.at[0], 1)

    all_chips(send_a, 0, z_n)

    @pl.when(core == 1)
    def _():
        pl.semaphore_wait(sem_known.at[1], 1)
        tell_other_core(sem_known.at[1])
        pl.semaphore_signal(sem_known.at[2], inc=1, device_id=other_ch)

    @pl.when(core == 0)
    def _():
        pl.semaphore_wait(sem_known.at[1], 1)

    all_chips(send_a, 1, 0)
    send_a(slot)

    p_row, p_col = iota((2 * r_n, 2 * n), 0), iota((2 * r_n, 2 * n), 1)
    first = (p_row & 1) * n + 3 * (p_row >> 1)
    for j in range(3):
        rows = dot(one_hot(p_col == first + j), x_ref[0 : 2 * n], 1, 0)
        ps[j] = rows.astype(BF16).reshape(r_n, 2, chans)
    p_row, p_col = iota((2 * r_n, n), 0), iota((2 * r_n, n), 1)
    last = x_ref[2 * n : 3 * n]
    rows = dot(one_hot(p_col == 3 * (p_row >> 1) + (p_row & 1)), last, 1, 0)
    ps[3] = rows.astype(BF16).reshape(r_n, 2, chans)
    rows = dot(one_hot(p_col == 3 * (p_row >> 1) + 2), last, 1, 0)
    ps[4] = rows.astype(BF16).reshape(r_n, 2, chans)

    to_core = lax.rem(c + core, 2)

    def send_p(s):
        r = 2 * s + to_core
        pltpu.make_async_remote_copy(
            src_ref=ps.at[:, r],
            dst_ref=pb.at[:, core * k_n + slot],
            send_sem=sem_p_send.at[0],
            recv_sem=sem_p_recv.at[0],
            device_id={"row": r, "ch": c},
        ).start()

    all_chips(send_p, 1, 0)
    all_chips(send_p, 0, 1)

    @pl.when(c == 0)
    def _():
        pltpu.make_async_copy(
            ps.at[:, me], pb.at[:, core * k_n + slot], sem_p_recv.at[0]
        ).start()

    @pl.when(c == 1)
    def _():
        send_p(slot)

    s_row, s_col = iota((n, n), 0), iota((n, n), 1)
    sixth = (s_col * 10923) >> 16
    left_at = 6 * sixth + ((s_col - 6 * sixth) >> 1)
    is_left = (s_col & 1) == 0
    sel_own = one_hot((s_row == left_at + 3 * (1 - core)) & is_left)
    sel_other = one_hot((s_row == left_at + 3 * core) & is_left)
    s_row, s_col = iota((2 * r_n, n), 0), iota((2 * r_n, n), 1)
    in_two = s_row < r_n
    s_two = jnp.where(in_two, s_row, s_row - r_n)
    sel_right = one_hot(
        s_col == 6 * (s_two >> 1) + jnp.where(in_two, 2 * (s_two & 1) + 1, 5)
    )

    for g in range(GROUPS):
        part = d.at[1 - core, :, g * per : (g + 1) * per]
        pltpu.make_async_copy(part, part, sem_a_recv.at[g]).wait()
        pltpu.make_async_remote_copy(
            src_ref=part,
            dst_ref=part,
            send_sem=sem_f_send,
            recv_sem=sem_f_recv.at[g],
            device_id=other_core,
        ).start()

    owns = [d[1 - core, lb].reshape(n, b) for lb in range(3)]
    own_left = [dot(sel_own, own, 1, 0) for own in owns]
    right = jnp.concatenate([dot(sel_right, own, 1, 0).astype(BF16) for own in owns], 1)
    for g in range(GROUPS):
        part = d.at[core, :, g * per : (g + 1) * per]
        pltpu.make_async_copy(part, part, sem_f_recv.at[g]).wait()
    lefts = []
    for lb in range(3):
        acc = own_left[lb] + dot(sel_other, d[core, lb].reshape(n, b), 1, 0)
        lefts.append(acc.astype(BF16))
    triangle = dot(right, jnp.concatenate(lefts, 1), 1, 1)
    upper, lower = triangle[:r_n], triangle[r_n:]
    for ib in range(3):
        sc[ib] = upper[:, ib * b : (ib + 1) * b].astype(BF16).reshape(k_n, 2, b)
    odd = (iota((r_n, b), 0) & 1) == 1
    sc[3] = jnp.where(odd, lower[:, b : 2 * b], lower[:, :b]).astype(BF16).reshape(k_n, 2, b)
    sc[4] = lower[:, 2 * b :].astype(BF16).reshape(k_n, 2, b)

    k_me = c * k_n + slot

    def send_c(index, to_ch):
        def send(s):
            pltpu.make_async_remote_copy(
                src_ref=sc.at[:, s],
                dst_ref=q.at[:, k_me],
                send_sem=sem_c_send.at[index],
                recv_sem=sem_c_recv,
                device_id={"row": 2 * s + 1 - core, "ch": to_ch},
            ).start()

        return send


    @pl.when(core == 1)
    def _():
        pl.semaphore_wait(sem_known.at[2], 1)
        tell_other_core(sem_known.at[2])

    @pl.when(core == 0)
    def _():
        pl.semaphore_wait(sem_known.at[2], 1)

    all_chips(send_c(1, 1 - c), 0, 0)
    all_chips(send_c(1, 1 - c), 1, 0)
    all_chips(send_c(0, c), 1, 0)
    all_chips(send_c(0, c), 0, 0)

    for copy in copies[8:]:
        copy.wait()
    mine = pb.at[:, pl.ds(to_core * k_n, k_n)]
    theirs = pb.at[:, pl.ds((1 - to_core) * k_n, k_n)]
    pltpu.make_async_copy(mine, mine, sem_p_recv.at[0]).wait()
    pltpu.make_async_remote_copy(
        src_ref=mine,
        dst_ref=mine,
        send_sem=sem_p_send.at[1],
        recv_sem=sem_p_recv.at[1],
        device_id=other_ch,
    ).start()
    s_row, s_col = iota((2 * r_n, n), 0), iota((2 * r_n, n), 1)
    source = s_row >> 1
    base = jnp.where(source < k_n, 6 * source, 6 * source - 6 * k_n + 3)
    sel_two = one_hot(s_col == base + (s_row & 1))
    third = s_col == base + 2
    sel_last = [one_hot(third & ((s_row & 1) == s)) for s in range(2)]
    gain_c = to_column(in_gain[...])
    pltpu.make_async_copy(theirs, theirs, sem_p_recv.at[1]).wait()
    for j in range(3):
        rest = pb[3 + j // 2].reshape(2 * r_n, chans)
        cells = dot(pb[j].reshape(2 * r_n, chans), sel_two, 0, 0) + dot(rest, sel_last[j % 2], 0, 0)
        pair_buf[j] = cells
        normed = normalize(cells, gain_c, 0).astype(BF16)
        gate_buf[j] = jax.nn.sigmoid(dot(wg[...], normed, 0, 0))

    hidden = wo.shape[0]
    p_row, p_col = iota((2 * hidden, hidden), 0), iota((2 * hidden, hidden), 1)
    twice = (p_row >> 1) == p_col
    gain_col = jnp.sum(jnp.where(twice, mid_gain[...], 0.0), 1, keepdims=True)
    w_twice = dot(wo[...], one_hot(twice), 0, 1)
    even = (iota((chans, 2 * hidden), 1) & 1) == 0
    w_out = jnp.concatenate(
        [jnp.where(even, w_twice, 0.0), jnp.where(even, 0.0, w_twice)], 0
    ).astype(BF16)
    gain_all = jnp.broadcast_to(gain_col, (2 * hidden, b)).reshape(2 * hidden // 8, 8, b)

    pltpu.make_async_copy(q, q, sem_c_recv).wait()

    tiles = 2 * hidden // 8

    def mean(v):
        t = jnp.sum(v, 0)
        t = t + pltpu.roll(t, 4, 0)
        return (t + pltpu.roll(t, 2, 0)) * (1.0 / hidden)

    next_c = to_column(next_gain[...])

    def finish(j, ib, update):
        span = slice(ib * b, (ib + 1) * b)
        new = (pair_buf[j, :, span] + gate_buf[j, :, span] * update).astype(BF16)
        values = new.astype(F32)
        normed = normalize(values, next_c, 0)
        second = c == 1
        out_pair[j, :, span] = jnp.where(second, values[half:], values[:half]).astype(BF16)
        out_norm[j, :, span] = jnp.where(second, normed[half:], normed[:half]).astype(BF16)

    for w in range(5):
        t = q[w].reshape(2 * hidden, b).astype(F32).reshape(tiles, 8, b)
        centred = t - mean(t)[None]
        scale = lax.rsqrt(mean(centred * centred) + EPS)[None]
        tri = (centred * scale * gain_all).astype(BF16).reshape(2 * hidden, b)
        update = dot(w_out, tri, 1, 0)
        if w < 3:
            finish(0, w, update[:chans])
            finish(1, w, update[chans:])
        elif w == 3:
            finish(2, 0, update[:chans])
            finish(2, 1, update[chans:])
        else:
            finish(2, 2, update[:chans])

    pltpu.make_async_copy(sa, sa, sem_a_send).wait()
    part = d.at[1 - core]
    pltpu.make_async_copy(part, part, sem_f_send).wait()

    @pl.when(c == 0)
    def _():
        part = ps.at[:, 0 : k_n - 1]
        pltpu.make_async_copy(part, part, sem_p_send.at[0]).wait()

    @pl.when(c == 1)
    def _():
        part = ps.at[:, 0:k_n]
        pltpu.make_async_copy(part, part, sem_p_send.at[0]).wait()

    pltpu.make_async_copy(mine, mine, sem_p_send.at[1]).wait()
    pltpu.make_async_copy(sc, sc, sem_c_send.at[0]).wait()
    pltpu.make_async_copy(sc, sc, sem_c_send.at[1]).wait()


def local(
    r_n,
    pair_rep,
    res_mask,
    in_gain,
    w_left,
    w_left_gate,
    w_right,
    w_right_gate,
    w_gate,
    mid_gain,
    w_out,
    next_gain,
):
    rows, n, chans = pair_rep.shape
    k_n = r_n // 2
    half = chans // 2
    hl = w_left.shape[1]
    vmem = pl.BlockSpec(memory_space=pltpu.VMEM)
    place = pl.BlockSpec(memory_space=pltpu.HBM)
    dma = pltpu.SemaphoreType.DMA
    out = jax.ShapeDtypeStruct((3, half, n), BF16)
    new_pair, new_norm = pl.pallas_call(
        functools.partial(kernel, r_n),
        out_shape=(out, out),
        in_specs=[place] * 11,
        out_specs=(vmem, vmem),
        scratch_shapes=[
            pltpu.VMEM((rows * n, chans), BF16),
            pltpu.SMEM((n,), jnp.int32),
            pltpu.VMEM((n,), jnp.int32),
            pltpu.VMEM((1, chans), F32),
            pltpu.VMEM((hl, chans), BF16),
            pltpu.VMEM((hl, chans), BF16),
            pltpu.VMEM((hl, chans), BF16),
            pltpu.VMEM((hl, chans), BF16),
            pltpu.VMEM((chans, chans), BF16),
            pltpu.VMEM((1, r_n), F32),
            pltpu.VMEM((r_n, chans), BF16),
            pltpu.VMEM((1, chans), F32),
            pltpu.VMEM((k_n, 3, 3, 2, r_n), BF16),
            pltpu.VMEM((2, 3, k_n, 3, 2, r_n), BF16),
            pltpu.VMEM((5, r_n, 2, chans), BF16),
            pltpu.VMEM((5, r_n, 2, chans), BF16),
            pltpu.VMEM((5, k_n, 2, r_n), BF16),
            pltpu.VMEM((5, r_n, 2, r_n), BF16),
            pltpu.VMEM((3, chans, n), F32),
            pltpu.VMEM((3, chans, n), F32),
            dma((12,)),
            pltpu.SemaphoreType.REGULAR((3,)),
            dma,
            dma((GROUPS,)),
            dma,
            dma((GROUPS,)),
            dma((2,)),
            dma((2,)),
            dma((2,)),
            dma,
        ],
        compiler_params=pltpu.CompilerParams(
            collective_id=0, has_side_effects=True, vmem_limit_bytes=8 * 1024 * 1024
        ),
    )(
        *(
            pltpu.with_memory_space_constraint(a, pltpu.HBM)
            for a in (
                pair_rep.reshape(rows * n, chans),
                res_mask,
                in_gain.reshape(1, chans),
                w_left.T,
                w_left_gate.T,
                w_right.T,
                w_right_gate.T,
                w_gate,
                mid_gain.reshape(1, -1),
                w_out,
                next_gain.reshape(1, chans),
            )
        )
    )
    return jnp.transpose(new_pair, (2, 0, 1)), jnp.transpose(new_norm, (2, 0, 1))


def solution(mesh):
    return jax.shard_map(
        functools.partial(local, mesh.shape["row"]),
        mesh=mesh,
        in_specs=(
            P("row", None, None),
            P(),
            P(),
            P(None, "ch"),
            P(None, "ch"),
            P(None, "ch"),
            P(None, "ch"),
            P(),
            P(),
            P(),
            P(),
        ),
        out_specs=(P(None, "row", "ch"), P(None, "row", "ch")),
        check_vma=False,
    )
```

```python
import functools

import jax
import jax.numpy as jnp
from jax import lax
from jax.experimental import pallas as pl
from jax.experimental.pallas import tpu as pltpu
from jax.sharding import PartitionSpec as P

EPS = 1e-05
F32 = jnp.float32
BF16 = jnp.bfloat16
GROUPS = 8


def dot(a, b, ca, cb):
    return lax.dot_general(a, b, (((ca,), (cb,)), ((), ())), preferred_element_type=F32)


def iota(shape, dim):
    return lax.broadcasted_iota(jnp.int32, shape, dim)


def one_hot(cond):
    return jnp.where(cond, 1.0, 0.0).astype(BF16)


def to_column(row):
    size = row.shape[1]
    diagonal = iota((size, size), 0) == iota((size, size), 1)
    return jnp.sum(jnp.where(diagonal, row, 0.0), 1, keepdims=True)


def normalize(v, gain, along):
    scale = 1.0 / v.shape[along]
    centred = v - jnp.sum(v, along, keepdims=True) * scale
    var = jnp.sum(centred * centred, along, keepdims=True) * scale
    return centred * lax.rsqrt(var + EPS) * gain


def kernel(
    rows_n,
    x_any,
    mask_any,
    in_any,
    wl_any,
    wlg_any,
    wr_any,
    wrg_any,
    wg_any,
    mid_any,
    wo_any,
    next_any,
    out_pair,
    out_norm,
    x_ref,
    mask_smem,
    mask_row,
    in_gain,
    wl,
    wlg,
    wr,
    wrg,
    wg,
    mid_gain,
    wo,
    next_gain,
    sa,
    d,
    ps,
    pb,
    sc,
    q,
    gate_buf,
    pair_buf,
    sem_in,
    sem_known,
    sem_a_send,
    sem_a_recv,
    sem_f_send,
    sem_f_recv,
    sem_p_send,
    sem_p_recv,
    sem_c_send,
    sem_c_recv,
):
    r_n = rows_n
    k_n = r_n // 2
    n = 3 * r_n
    b = r_n
    chans = x_ref.shape[1]
    half = chans // 2
    me = lax.axis_index("row")
    c = lax.axis_index("ch")
    core = lax.rem(me, 2)
    slot = me // 2
    per = k_n // GROUPS
    x_n = 4 if r_n >= 128 else 2
    z_n = k_n // (2 * x_n)
    at_x = lax.rem(slot, x_n)
    at_y = lax.rem(slot // x_n, 2)
    at_z = slot // (2 * x_n)

    ahead = 1 - 2 * core
    planes = [
        lax.rem(at_z + z_n + ((u + 1) // 2) * (ahead if u % 2 else -ahead), z_n) * (2 * x_n)
        for u in range(z_n)
    ]

    def column(dy, dx):
        return lax.rem(at_y + dy, 2) * x_n + lax.rem(at_x + dx, x_n)

    here = column(0, 0)

    def tell(sem, chip):
        pl.semaphore_signal(sem, inc=1, device_id={"row": 2 * chip + 1, "ch": c})

    def tell_row(sem):
        for t in range(1, x_n):
            tell(sem, planes[0] + column(0, t))

    def all_chips(send, dy, last):
        def some(t, carry):
            to = column(dy, x_n - 1 - t)
            for u in reversed(range(z_n)):
                send(planes[u] + to)
            return carry

        lax.fori_loop(0, x_n - 1, some, 0)
        for u in reversed(range(last, z_n)):
            send(planes[u] + column(dy, 0))

    barrier = pltpu.get_barrier_semaphore()
    other_core = {"row": 2 * slot + 1 - core, "ch": c}
    other_ch = {"row": me, "ch": 1 - c}

    def tell_other_core(sem):
        pl.semaphore_signal(sem, inc=1, device_id=other_core)

    for u in reversed(range(1, z_n)):
        tell(barrier, planes[u] + here)
    tell_row(barrier)
    tell(barrier, planes[0] + column(1, 0))

    @pl.when(core == 0)
    def _():
        tell_other_core(barrier)

    @pl.when(core == 1)
    def _():
        pl.semaphore_signal(barrier, inc=1, device_id=other_ch)

    arrays = (
        (x_any, x_ref),
        (wl_any, wl),
        (wlg_any, wlg),
        (wr_any, wr),
        (wrg_any, wrg),
        (in_any, in_gain),
        (mask_any, mask_smem),
        (mask_any, mask_row),
        (wg_any, wg),
        (mid_any, mid_gain),
        (wo_any, wo),
        (next_any, next_gain),
    )
    copies = [
        pltpu.make_async_copy(src, dst, sem_in.at[i]) for i, (src, dst) in enumerate(arrays)
    ]
    for copy in copies:
        copy.start()
    for copy in copies[:8]:
        copy.wait()

    hl = wl.shape[0]
    p_row, p_col = iota((2 * hl, hl), 0), iota((2 * hl, hl), 1)
    to_left, to_right = one_hot(p_row == 2 * p_col), one_hot(p_row == 2 * p_col + 1)
    w_lin = (dot(to_left, wl[...], 1, 0) + dot(to_right, wr[...], 1, 0)).astype(BF16)
    w_switch = (dot(to_left, wlg[...], 1, 0) + dot(to_right, wrg[...], 1, 0)).astype(BF16)
    group = slot // per

    def project(i):
        normed = normalize(x_ref[i * n : (i + 1) * n].astype(F32), in_gain[...], 1).astype(BF16)
        lin = dot(w_lin, normed, 1, 1)
        switch = dot(w_switch, normed, 1, 1)
        mask = mask_row[...].reshape(1, n).astype(F32) * mask_smem[3 * me + i].astype(F32)
        sides = (jax.nn.sigmoid(switch) * lin * mask).astype(BF16)
        for lb in range(3):
            sa[:, lb, i] = sides[:, lb * b : (lb + 1) * b].reshape(hl, 2, b)

    project(0)
    project(1)
    @pl.when(core == 1)
    def _():
        pl.semaphore_wait(barrier, 2 * (z_n + x_n - 1) + 2)
        tell_row(sem_known.at[0])
        tell_other_core(barrier)

    @pl.when(core == 0)
    def _():
        pl.semaphore_wait(barrier, 1)

    project(2)

    def send_a(s):
        pltpu.make_async_remote_copy(
            src_ref=sa.at[s],
            dst_ref=d.at[core, :, slot],
            send_sem=sem_a_send,
            recv_sem=sem_a_recv.at[group],
            device_id={"row": 2 * s + 1 - core, "ch": c},
        ).start()

    for u in reversed(range(1, z_n)):
        send_a(planes[u] + here)

    @pl.when(core == 1)
    def _():
        pl.semaphore_wait(sem_known.at[0], x_n - 1)
        tell(sem_known.at[1], planes[0] + column(1, 0))
        tell_other_core(sem_known.at[0])

    @pl.when(core == 0)
    def _():
        pl.semaphore_wait(sem_known.at[0], 1)

    all_chips(send_a, 0, z_n)

    @pl.when(core == 1)
    def _():
        pl.semaphore_wait(sem_known.at[1], 1)
        tell_other_core(sem_known.at[1])
        pl.semaphore_signal(sem_known.at[2], inc=1, device_id=other_ch)

    @pl.when(core == 0)
    def _():
        pl.semaphore_wait(sem_known.at[1], 1)

    all_chips(send_a, 1, 0)
    send_a(slot)

    p_row, p_col = iota((2 * r_n, 2 * n), 0), iota((2 * r_n, 2 * n), 1)
    first = (p_row & 1) * n + 3 * (p_row >> 1)
    for j in range(3):
        rows = dot(one_hot(p_col == first + j), x_ref[0 : 2 * n], 1, 0)
        ps[j] = rows.astype(BF16).reshape(r_n, 2, chans)
    p_row, p_col = iota((2 * r_n, n), 0), iota((2 * r_n, n), 1)
    last = x_ref[2 * n : 3 * n]
    rows = dot(one_hot(p_col == 3 * (p_row >> 1) + (p_row & 1)), last, 1, 0)
    ps[3] = rows.astype(BF16).reshape(r_n, 2, chans)
    rows = dot(one_hot(p_col == 3 * (p_row >> 1) + 2), last, 1, 0)
    ps[4] = rows.astype(BF16).reshape(r_n, 2, chans)

    to_core = lax.rem(c + core, 2)

    def send_p(s):
        r = 2 * s + to_core
        pltpu.make_async_remote_copy(
            src_ref=ps.at[:, r],
            dst_ref=pb.at[:, core * k_n + slot],
            send_sem=sem_p_send.at[0],
            recv_sem=sem_p_recv.at[0],
            device_id={"row": r, "ch": c},
        ).start()

    all_chips(send_p, 1, 0)
    all_chips(send_p, 0, 1)

    @pl.when(c == 0)
    def _():
        pltpu.make_async_copy(
            ps.at[:, me], pb.at[:, core * k_n + slot], sem_p_recv.at[0]
        ).start()

    @pl.when(c == 1)
    def _():
        send_p(slot)

    s_row, s_col = iota((n, n), 0), iota((n, n), 1)
    sixth = (s_col * 10923) >> 16
    left_at = 6 * sixth + ((s_col - 6 * sixth) >> 1)
    is_left = (s_col & 1) == 0
    sel_own = one_hot((s_row == left_at + 3 * (1 - core)) & is_left)
    sel_other = one_hot((s_row == left_at + 3 * core) & is_left)
    s_row, s_col = iota((2 * r_n, n), 0), iota((2 * r_n, n), 1)
    in_two = s_row < r_n
    s_two = jnp.where(in_two, s_row, s_row - r_n)
    sel_right = one_hot(
        s_col == 6 * (s_two >> 1) + jnp.where(in_two, 2 * (s_two & 1) + 1, 5)
    )

    for g in range(GROUPS):
        part = d.at[1 - core, :, g * per : (g + 1) * per]
        pltpu.make_async_copy(part, part, sem_a_recv.at[g]).wait()
        pltpu.make_async_remote_copy(
            src_ref=part,
            dst_ref=part,
            send_sem=sem_f_send,
            recv_sem=sem_f_recv.at[g],
            device_id=other_core,
        ).start()

    owns = [d[1 - core, lb].reshape(n, b) for lb in range(3)]
    own_left = [dot(sel_own, own, 1, 0) for own in owns]
    right = jnp.concatenate([dot(sel_right, own, 1, 0).astype(BF16) for own in owns], 1)
    for g in range(GROUPS):
        part = d.at[core, :, g * per : (g + 1) * per]
        pltpu.make_async_copy(part, part, sem_f_recv.at[g]).wait()
    lefts = []
    for lb in range(3):
        acc = own_left[lb] + dot(sel_other, d[core, lb].reshape(n, b), 1, 0)
        lefts.append(acc.astype(BF16))
    triangle = dot(right, jnp.concatenate(lefts, 1), 1, 1)
    upper, lower = triangle[:r_n], triangle[r_n:]
    for ib in range(3):
        sc[ib] = upper[:, ib * b : (ib + 1) * b].astype(BF16).reshape(k_n, 2, b)
    odd = (iota((r_n, b), 0) & 1) == 1
    sc[3] = jnp.where(odd, lower[:, b : 2 * b], lower[:, :b]).astype(BF16).reshape(k_n, 2, b)
    sc[4] = lower[:, 2 * b :].astype(BF16).reshape(k_n, 2, b)

    k_me = c * k_n + slot

    def send_c(index, to_ch):
        def send(s):
            pltpu.make_async_remote_copy(
                src_ref=sc.at[:, s],
                dst_ref=q.at[:, k_me],
                send_sem=sem_c_send.at[index],
                recv_sem=sem_c_recv,
                device_id={"row": 2 * s + 1 - core, "ch": to_ch},
            ).start()

        return send


    @pl.when(core == 1)
    def _():
        pl.semaphore_wait(sem_known.at[2], 1)
        tell_other_core(sem_known.at[2])

    @pl.when(core == 0)
    def _():
        pl.semaphore_wait(sem_known.at[2], 1)

    all_chips(send_c(1, 1 - c), 0, 0)
    all_chips(send_c(1, 1 - c), 1, 0)
    all_chips(send_c(0, c), 1, 0)
    all_chips(send_c(0, c), 0, 0)

    for copy in copies[8:]:
        copy.wait()
    mine = pb.at[:, pl.ds(to_core * k_n, k_n)]
    theirs = pb.at[:, pl.ds((1 - to_core) * k_n, k_n)]
    pltpu.make_async_copy(mine, mine, sem_p_recv.at[0]).wait()
    pltpu.make_async_remote_copy(
        src_ref=mine,
        dst_ref=mine,
        send_sem=sem_p_send.at[1],
        recv_sem=sem_p_recv.at[1],
        device_id=other_ch,
    ).start()
    s_row, s_col = iota((2 * r_n, n), 0), iota((2 * r_n, n), 1)
    source = s_row >> 1
    base = jnp.where(source < k_n, 6 * source, 6 * source - 6 * k_n + 3)
    sel_two = one_hot(s_col == base + (s_row & 1))
    third = s_col == base + 2
    sel_last = [one_hot(third & ((s_row & 1) == s)) for s in range(2)]
    gain_c = to_column(in_gain[...])
    pltpu.make_async_copy(theirs, theirs, sem_p_recv.at[1]).wait()
    for j in range(3):
        rest = pb[3 + j // 2].reshape(2 * r_n, chans)
        cells = dot(pb[j].reshape(2 * r_n, chans), sel_two, 0, 0) + dot(rest, sel_last[j % 2], 0, 0)
        pair_buf[j] = cells
        normed = normalize(cells, gain_c, 0).astype(BF16)
        gate_buf[j] = jax.nn.sigmoid(dot(wg[...], normed, 0, 0))

    hidden = wo.shape[0]
    p_row, p_col = iota((2 * hidden, hidden), 0), iota((2 * hidden, hidden), 1)
    twice = (p_row >> 1) == p_col
    gain_col = jnp.sum(jnp.where(twice, mid_gain[...], 0.0), 1, keepdims=True)
    w_twice = dot(wo[...], one_hot(twice), 0, 1)
    even = (iota((chans, 2 * hidden), 1) & 1) == 0
    w_out = jnp.concatenate(
        [jnp.where(even, w_twice, 0.0), jnp.where(even, 0.0, w_twice)], 0
    ).astype(BF16)
    gain_all = jnp.broadcast_to(gain_col, (2 * hidden, b)).reshape(2 * hidden // 8, 8, b)

    pltpu.make_async_copy(q, q, sem_c_recv).wait()

    tiles = 2 * hidden // 8

    def mean(v):
        t = jnp.sum(v, 0)
        t = t + pltpu.roll(t, 4, 0)
        return (t + pltpu.roll(t, 2, 0)) * (1.0 / hidden)

    next_c = to_column(next_gain[...])

    def finish(j, ib, update):
        span = slice(ib * b, (ib + 1) * b)
        new = (pair_buf[j, :, span] + gate_buf[j, :, span] * update).astype(BF16)
        values = new.astype(F32)
        normed = normalize(values, next_c, 0)
        second = c == 1
        out_pair[j, :, span] = jnp.where(second, values[half:], values[:half]).astype(BF16)
        out_norm[j, :, span] = jnp.where(second, normed[half:], normed[:half]).astype(BF16)

    for w in range(5):
        t = q[w].reshape(2 * hidden, b).astype(F32).reshape(tiles, 8, b)
        centred = t - mean(t)[None]
        scale = lax.rsqrt(mean(centred * centred) + EPS)[None]
        tri = (centred * scale * gain_all).astype(BF16).reshape(2 * hidden, b)
        update = dot(w_out, tri, 1, 0)
        if w < 3:
            finish(0, w, update[:chans])
            finish(1, w, update[chans:])
        elif w == 3:
            finish(2, 0, update[:chans])
            finish(2, 1, update[chans:])
        else:
            finish(2, 2, update[:chans])

    pltpu.make_async_copy(sa, sa, sem_a_send).wait()
    part = d.at[1 - core]
    pltpu.make_async_copy(part, part, sem_f_send).wait()

    @pl.when(c == 0)
    def _():
        part = ps.at[:, 0 : k_n - 1]
        pltpu.make_async_copy(part, part, sem_p_send.at[0]).wait()

    @pl.when(c == 1)
    def _():
        part = ps.at[:, 0:k_n]
        pltpu.make_async_copy(part, part, sem_p_send.at[0]).wait()

    pltpu.make_async_copy(mine, mine, sem_p_send.at[1]).wait()
    pltpu.make_async_copy(sc, sc, sem_c_send.at[0]).wait()
    pltpu.make_async_copy(sc, sc, sem_c_send.at[1]).wait()


def local(
    r_n,
    pair_rep,
    res_mask,
    in_gain,
    w_left,
    w_left_gate,
    w_right,
    w_right_gate,
    w_gate,
    mid_gain,
    w_out,
    next_gain,
):
    rows, n, chans = pair_rep.shape
    k_n = r_n // 2
    half = chans // 2
    hl = w_left.shape[1]
    vmem = pl.BlockSpec(memory_space=pltpu.VMEM)
    place = pl.BlockSpec(memory_space=pltpu.HBM)
    dma = pltpu.SemaphoreType.DMA
    out = jax.ShapeDtypeStruct((3, half, n), BF16)
    new_pair, new_norm = pl.pallas_call(
        functools.partial(kernel, r_n),
        out_shape=(out, out),
        in_specs=[place] * 11,
        out_specs=(vmem, vmem),
        scratch_shapes=[
            pltpu.VMEM((rows * n, chans), BF16),
            pltpu.SMEM((n,), jnp.int32),
            pltpu.VMEM((n,), jnp.int32),
            pltpu.VMEM((1, chans), F32),
            pltpu.VMEM((hl, chans), BF16),
            pltpu.VMEM((hl, chans), BF16),
            pltpu.VMEM((hl, chans), BF16),
            pltpu.VMEM((hl, chans), BF16),
            pltpu.VMEM((chans, chans), BF16),
            pltpu.VMEM((1, r_n), F32),
            pltpu.VMEM((r_n, chans), BF16),
            pltpu.VMEM((1, chans), F32),
            pltpu.VMEM((k_n, 3, 3, 2, r_n), BF16),
            pltpu.VMEM((2, 3, k_n, 3, 2, r_n), BF16),
            pltpu.VMEM((5, r_n, 2, chans), BF16),
            pltpu.VMEM((5, r_n, 2, chans), BF16),
            pltpu.VMEM((5, k_n, 2, r_n), BF16),
            pltpu.VMEM((5, r_n, 2, r_n), BF16),
            pltpu.VMEM((3, chans, n), F32),
            pltpu.VMEM((3, chans, n), F32),
            dma((12,)),
            pltpu.SemaphoreType.REGULAR((3,)),
            dma,
            dma((GROUPS,)),
            dma,
            dma((GROUPS,)),
            dma((2,)),
            dma((2,)),
            dma((2,)),
            dma,
        ],
        compiler_params=pltpu.CompilerParams(
            collective_id=0, has_side_effects=True, vmem_limit_bytes=8 * 1024 * 1024
        ),
    )(
        *(
            pltpu.with_memory_space_constraint(a, pltpu.HBM)
            for a in (
                pair_rep.reshape(rows * n, chans),
                res_mask,
                in_gain.reshape(1, chans),
                w_left.T,
                w_left_gate.T,
                w_right.T,
                w_right_gate.T,
                w_gate,
                mid_gain.reshape(1, -1),
                w_out,
                next_gain.reshape(1, chans),
            )
        )
    )
    return jnp.transpose(new_pair, (2, 0, 1)), jnp.transpose(new_norm, (2, 0, 1))


def solution(mesh):
    return jax.shard_map(
        functools.partial(local, mesh.shape["row"]),
        mesh=mesh,
        in_specs=(
            P("row", None, None),
            P(),
            P(),
            P(None, "ch"),
            P(None, "ch"),
            P(None, "ch"),
            P(None, "ch"),
            P(),
            P(),
            P(),
            P(),
        ),
        out_specs=(P(None, "row", "ch"), P(None, "row", "ch")),
        check_vma=False,
    )
```
